32 devices in a mesh: groups: 2 (over x), seq: 8 (over z, y), head: 2 (over core).
Axes of the slice: x: 2, y: 2, z: 4, core: 2. Of those that a mesh axis runs over, the one named last changes fastest.
Arguments:
- queries: bfloat16 [4096, 32, 192], P(('groups', 'seq'), 'head'), parts along dimension 0, may hold values from -8 to 8
- keys: bfloat16 [4096, 4, 192], P(('groups', 'seq'), 'head'), parts along dimension 0, may hold values from -8 to 8
- values: bfloat16 [4096, 4, 128], P(('groups', 'seq'), 'head'), parts along dimension 0, may hold values from -6 to 6
- lists: int32 [64, 4, 16], P(('groups', 'seq'), 'head'), parts along dimension 0, may hold values from -1 to 31, as said below
- gate_weight: bfloat16 [32, 192, 3], P('head'), may hold values from -0.4375 to 0.4375
- pool_key: float32 [32, 4, 192], P(None, 'head'), may hold values from 0.08 to 0.3
- pool_value: float32 [32, 4, 128], P(None, 'head'), may hold values from 0.08 to 0.3
- out_weight: bfloat16 [2560, 4096], P(None, 'head'), may hold values from -0.09375 to 0.09375
Outputs:
- attended: bfloat16 [4096, 2560], P(('groups', 'seq'), 'head'), parts along dimension 0
The draws below stay inside these ranges and needn't reach their ends.
There are 2 independent parts, one for each index of `groups`. The reference program is written for one: setup_inputs(seed, part) draws one part's arguments, and reference() takes and returns one part's arrays. A program takes and returns all parts, laid end to end along the dimension named above; an argument that names none is the same for every part. Nothing has to cross between parts.
Inputs may be any that keep to these rules, and one draw needn't show every extreme that they name: `lists`: each entry is a block index of 64 tokens or -1 for an empty entry. The valid entries of one list are distinct, never lie after the tile's own block, and always include block 0, the tile's own block and the block before it. Over the tiles of one device's 256 tokens and one group, the valid entries that lie in any one other device's shard name at most 2 distinct blocks.
All inputs are finite; a program needn't handle non-finite values.
Results may differ from the reference program's by a relative error of at most 0.012.
Values may be sent and summed in bfloat16 or wider, within the bound.
A program may use at most 192 MiB of HBM per device.

```python
import math
import jax
import jax.numpy as jnp
from jax import lax

D = 2560
HEADS = 32
GROUPS = 4
DQ = 192
DV = 128
BLOCK = 64
CBLOCK = 32
STRIDE = 16
TOP = 16
SLOTS = 2
WINDOW = 256
TOK_DEV = 256
HPG = 8
SEQLEN = 2048
NTILES = 32
N_SEQ = 8


def draw_queries(key, part):
    shape = (SEQLEN, HEADS, DQ)
    base = jnp.clip(jax.random.normal(jax.random.fold_in(key, 1), shape, jnp.float32), -8.0, 8.0)
    return base.astype(jnp.bfloat16)


def draw_keys(key, part):
    shape = (SEQLEN, GROUPS, DQ)
    base = jnp.clip(jax.random.normal(jax.random.fold_in(key, 3), shape, jnp.float32), -8.0, 8.0)
    return base.astype(jnp.bfloat16)


def draw_lists(key, part):
    blocks_dev = TOK_DEV // BLOCK
    offs = jnp.arange(blocks_dev, dtype=jnp.int32)
    owners = jnp.arange(N_SEQ, dtype=jnp.int32)
    device_axis = owners[:, None, None, None]
    owner_axis = owners[None, None, :, None]
    pick_score = jax.random.randint(jax.random.fold_in(key, 11), (N_SEQ, GROUPS, N_SEQ, blocks_dev), 0, 1 << 12) * blocks_dev + offs
    pick_score = jnp.where((owner_axis == device_axis - 1) & (offs == blocks_dev - 1), 1 << 28, pick_score)
    pick_score = jnp.where((owner_axis == 0) & (offs == 0), 1 << 29, pick_score)
    ignored, slot_offs = lax.top_k(pick_score, SLOTS)
    allowed = (owner_axis * blocks_dev + slot_offs).reshape(N_SEQ, GROUPS, N_SEQ * SLOTS)
    tile = jnp.arange(NTILES, dtype=jnp.int32)
    device_of_tile = tile // blocks_dev
    local_of_tile = tile % blocks_dev
    table = allowed[device_of_tile]
    own_blocks = device_of_tile[:, None] * blocks_dev + offs[None, :]
    own_blocks = jnp.broadcast_to(own_blocks[:, None, :], (NTILES, GROUPS, blocks_dev))
    candidate = jnp.concatenate([table, own_blocks], 2)
    width = N_SEQ * SLOTS + blocks_dev
    column = jnp.arange(width, dtype=jnp.int32)[None, None, :]
    usable = jnp.where(column < N_SEQ * SLOTS, column // SLOTS < device_of_tile[:, None, None], column - N_SEQ * SLOTS <= local_of_tile[:, None, None])
    noise = jax.random.randint(jax.random.fold_in(key, 12), (NTILES, GROUPS, width), 0, 1 << 16)
    here = tile[:, None, None]
    forced = (candidate == 0) | (candidate == here) | (candidate == here - 1)
    score = jnp.where(forced, 1 << 20, noise) * width + column
    score = jnp.where(usable, score, -1 - column)
    ignored, chosen = lax.top_k(score, TOP)
    okay = jnp.take_along_axis(usable, chosen, axis=2)
    block = jnp.take_along_axis(candidate, chosen, axis=2)
    return jnp.where(okay, block, -1).astype(jnp.int32)


def shard_levels(stream_key, extent, shards, smallest, largest):
    def one(axis_at, blocks):
        heights = jax.random.uniform(jax.random.fold_in(jax.random.fold_in(stream_key, 6), axis_at), (blocks,), jnp.float32, smallest / len(shards), largest / len(shards))
        return jnp.repeat(jnp.exp(heights), extent[axis_at] // blocks).reshape((-1,) + (1,) * (len(extent) - axis_at - 1))

    gain = one(*shards[0])
    for cut in shards[1:]:
        gain = gain * one(*cut)
    return gain


def normal_values(stream_key, shape, scale, most, cuts=(), held_as=jnp.bfloat16):
    drawn = jax.random.normal(stream_key, shape, jnp.float32) * scale
    if len(cuts) > 0:
        drawn = shard_levels(stream_key, shape, cuts, -0.22, 0.18) * drawn
    return jnp.clip(drawn, min=-most, max=most).astype(held_as)


def setup_inputs(seed: int = 0, part: int = 0) -> dict:
    streams_of = jax.random.split(jax.random.key(seed), 9)
    part_keys = jax.random.split(jax.random.fold_in(streams_of[8], part), 9)
    return {
        "queries": draw_queries(jax.random.fold_in(jax.random.fold_in(streams_of[8], part), 71), part),
        "keys": draw_keys(jax.random.fold_in(jax.random.fold_in(streams_of[8], part), 71), part),
        "values": normal_values(part_keys[2], (SEQLEN, GROUPS, DV), 1.0, 6.0, ((0, 8), (1, 2))),
        "lists": draw_lists(jax.random.fold_in(jax.random.fold_in(streams_of[8], part), 71), part),
        "gate_weight": normal_values(streams_of[4], (HEADS, DQ, 3), DQ ** -0.5, 0.4375, ((0, 2),)),
        "pool_key": jnp.clip(jnp.exp(math.log(0.3) - 1.3217559 * jax.random.uniform(streams_of[5], (CBLOCK, GROUPS, DQ), jnp.float32) ** shard_levels(streams_of[5], (CBLOCK, GROUPS, DQ), ((1, 2),), -0.2, 0.2)), 0.08, 0.3),
        "pool_value": jnp.clip(jnp.exp(math.log(0.3) - 1.3217559 * jax.random.uniform(streams_of[6], (CBLOCK, GROUPS, DV), jnp.float32) ** shard_levels(streams_of[6], (CBLOCK, GROUPS, DV), ((1, 2),), -0.2, 0.2)), 0.08, 0.3),
        "out_weight": normal_values(streams_of[7], (D, HEADS * DV), (HEADS * DV) ** -0.5, 0.09375, ((1, 2),)),
    }


def masked_weights(scores, mask):
    peak = jnp.max(jnp.where(mask, scores, -1e30), axis=-1, keepdims=True)
    raised = jnp.exp(jnp.where(mask, scores - peak, -1e30))
    total = jnp.sum(raised, axis=-1, keepdims=True)
    return (raised / jnp.maximum(total, 1.0)).astype(jnp.bfloat16)


def compress(raw, pool):
    count = raw.shape[0] // STRIDE
    tail = jnp.zeros((CBLOCK - STRIDE,) + raw.shape[1:], jnp.float32)
    padded = jnp.concatenate([raw.astype(jnp.float32), tail], 0)
    total = jnp.zeros((count,) + raw.shape[1:], jnp.float32)
    for part in range(CBLOCK // STRIDE):
        piece = padded[part * STRIDE:part * STRIDE + count * STRIDE].reshape((count, STRIDE) + raw.shape[1:])
        weights = pool[part * STRIDE:(part + 1) * STRIDE].astype(jnp.float32)
        total = total + jnp.einsum("csgd,sgd->cgd", piece, weights, precision=lax.Precision.HIGHEST)
    return total.astype(jnp.bfloat16)


def reference(queries, keys, values, lists, gate_weight, pool_key, pool_value, out_weight):
    length = queries.shape[0]
    scale = DQ ** -0.5
    q_rows = 512 if length % 512 == 0 else BLOCK
    tiles = q_rows // BLOCK
    comp_keys = compress(keys, pool_key).astype(jnp.float32)
    comp_values = compress(values, pool_value).astype(jnp.float32)
    comp_end = jnp.arange(comp_keys.shape[0], dtype=jnp.int32) * STRIDE + CBLOCK - 1
    front_k = jnp.zeros((WINDOW,) + keys.shape[1:], keys.dtype)
    front_v = jnp.zeros((WINDOW,) + values.shape[1:], values.dtype)
    pad_keys = jnp.concatenate([front_k, keys], 0)
    pad_values = jnp.concatenate([front_v, values], 0)
    gates = jax.nn.sigmoid(jnp.einsum("thd,hdb->thb", queries.astype(jnp.float32), gate_weight.astype(jnp.float32)))
    group_index = jnp.arange(GROUPS, dtype=jnp.int32)[None, :, None, None]
    offsets = jnp.arange(BLOCK, dtype=jnp.int32)

    def one_block(index):
        first = index * q_rows
        query = lax.dynamic_slice_in_dim(queries, first, q_rows, 0).astype(jnp.float32).reshape(q_rows, GROUPS, HPG, DQ)
        where_q = first + jnp.arange(q_rows, dtype=jnp.int32)
        scores = jnp.einsum("tghd,cgd->tghc", query, comp_keys) * scale
        mask = (comp_end[None, :] <= where_q[:, None])[:, None, None, :]
        weights = masked_weights(scores, mask)
        branch_c = jnp.einsum("tghc,cgd->tghd", weights.astype(jnp.float32), comp_values)

        listed = lax.dynamic_slice_in_dim(lists, index * tiles, tiles, 0)
        valid = listed >= 0
        rows = jnp.maximum(listed, 0)[..., None] * BLOCK + offsets
        chosen_keys = keys[rows, group_index].astype(jnp.float32)
        chosen_values = values[rows, group_index].astype(jnp.float32)
        tile_query = query.reshape(tiles, BLOCK, GROUPS, HPG, DQ)
        scores = jnp.einsum("atghd,agkrd->atghkr", tile_query, chosen_keys) * scale
        tile_where = where_q.reshape(tiles, BLOCK)
        mask = valid[:, None, :, None, :, None] & (rows[:, None, :, None, :, :] <= tile_where[:, :, None, None, None, None])
        scores = scores.reshape(tiles, BLOCK, GROUPS, HPG, TOP * BLOCK)
        mask = jnp.broadcast_to(mask, (tiles, BLOCK, GROUPS, 1, TOP, BLOCK)).reshape(tiles, BLOCK, GROUPS, 1, TOP * BLOCK)
        weights = masked_weights(scores, mask)
        branch_s = jnp.einsum("atghn,agnd->atghd", weights.astype(jnp.float32), chosen_values.reshape(tiles, GROUPS, TOP * BLOCK, DV))
        branch_s = branch_s.reshape(q_rows, GROUPS, HPG, DV)

        near_keys = lax.dynamic_slice_in_dim(pad_keys, first, WINDOW + q_rows, 0).astype(jnp.float32)
        near_values = lax.dynamic_slice_in_dim(pad_values, first, WINDOW + q_rows, 0).astype(jnp.float32)
        where_k = first - WINDOW + jnp.arange(WINDOW + q_rows, dtype=jnp.int32)
        mask = (where_k[None, :] >= 0) & (where_k[None, :] <= where_q[:, None]) & (where_k[None, :] > where_q[:, None] - WINDOW)
        scores = jnp.einsum("tghd,kgd->tghk", query, near_keys) * scale
        weights = masked_weights(scores, mask[:, None, None, :])
        branch_w = jnp.einsum("tghk,kgd->tghd", weights.astype(jnp.float32), near_values)

        gate = lax.dynamic_slice_in_dim(gates, first, q_rows, 0).reshape(q_rows, GROUPS, HPG, 3)
        mixed = gate[..., 0:1] * branch_c + gate[..., 1:2] * branch_s + gate[..., 2:3] * branch_w
        mixed = mixed.reshape(q_rows, HEADS * DV).astype(jnp.bfloat16)
        projected = lax.dot_general(mixed, out_weight, (((1,), (1,)), ((), ())), preferred_element_type=jnp.float32)
        return projected.astype(jnp.bfloat16)

    blocks = lax.map(one_block, jnp.arange(length // q_rows, dtype=jnp.int32))
    return blocks.reshape(length, out_weight.shape[0])
```

```python
import functools
import math

import jax
import jax.numpy as jnp
from jax import lax
from jax.experimental import pallas as pl
from jax.experimental.pallas import tpu as pltpu
from jax.sharding import PartitionSpec as P

BLOCK = 64
CBLOCK = 32
STRIDE = 16
WINDOW = 256
SLOTS = 2
LANES = 128
NONE = -1e30
FLOOR = -1e6
ONES = 16
MESH = pl.DeviceIdType.MESH


def mm(a, b):
    return jnp.dot(a, b, preferred_element_type=jnp.float32)


def flip(a):
    return jnp.transpose(a.astype(jnp.float32)).astype(jnp.bfloat16)


def kernel(
    n_seq, inner, factor, kcols,
    kv_ref, queries_ref, list_ref, gate_ref, poolk_ref, poolv_ref, w_ref, out_ref,
    kv, w, qt_ref, bias_ref, pool_ref, acc_s, acc_w, max_s, max_w, vt, near, front, back, mixed, gates, held_v, few_ref, kfew, vfew,
    outgo, incoming, held_s, held_p,
    own_sem, w_sem, zsend, ysend, recv, psend, precv,
):
    outer = n_seq // inner
    rows = kv.shape[1]
    heads = qt_ref.shape[0]
    groups = list_ref.shape[1]
    dq = queries_ref.shape[1]
    tiles = list_ref.shape[0]
    hpg = heads // groups
    dv = acc_s.shape[1] - ONES
    span = 2 * LANES
    blocks = rows // BLOCK
    per = rows // STRIDE
    me = lax.axis_index("seq")
    part = lax.axis_index("groups")
    side = lax.axis_index("head")
    z = me // inner
    y = me % inner

    own = pltpu.make_async_copy(kv_ref, kv.at[me], own_sem)
    own.start()
    weights = pltpu.make_async_copy(w_ref, w, w_sem)
    weights.start()

    barrier = pltpu.get_barrier_semaphore()

    def greet(who, hd):
        pl.semaphore_signal(barrier, inc=1, device_id=(part, who, hd), device_id_type=MESH)

    greet(me, 1 - side)

    @pl.when(z > 0)
    def _():
        greet(me - inner, side)

    @pl.when(z < outer - 1)
    def _():
        greet(me + inner, side)

    for e in range(1, inner):
        greet(z * inner + (y + e) % inner, side)
    lower = jnp.minimum(z, 1)
    upper = jnp.minimum(outer - 1 - z, 1)
    pl.semaphore_wait(barrier, inner + lower + upper)

    def along(s):
        return pltpu.make_async_remote_copy(
            src_ref=kv.at[s], dst_ref=kv.at[s], send_sem=zsend.at[s], recv_sem=recv.at[s],
            device_id=(part, me + inner, side), device_id_type=MESH)

    def across(s, e):
        return pltpu.make_async_remote_copy(
            src_ref=kv.at[s], dst_ref=kv.at[s], send_sem=ysend.at[s, e], recv_sem=recv.at[s],
            device_id=(part, z * inner + (y + e) % inner, side), device_id_type=MESH)

    def each_send(s, d, act):
        @pl.when(z < outer - 1)
        def _():
            act(along(s))

        for e in range(1, inner):
            @pl.when((d > 0) | (y + e < inner))
            def _():
                act(across(s, e))

    def arrive(s):
        pltpu.make_async_remote_copy(
            src_ref=kv.at[s], dst_ref=kv.at[s], send_sem=zsend.at[s], recv_sem=recv.at[s],
            device_id=(part, me, 1 - side), device_id_type=MESH).wait_recv()

    own.wait()
    each_send(me, 0, lambda copy: copy.start())

    key_at = lax.broadcasted_iota(jnp.int32, (rows, rows), 0)
    query_at = lax.broadcasted_iota(jnp.int32, (rows, rows), 1)
    front[...] = jnp.zeros_like(front)
    back[...] = jnp.zeros_like(back)
    vt[:, dv:, :] = jnp.ones((groups, ONES, rows), jnp.bfloat16)

    vfew[:, dv:, :] = jnp.ones((groups, ONES, vfew.shape[2]), jnp.bfloat16)
    for g in range(groups):
        cols = slice(g * dq, (g + 1) * dq)
        pool_ref[:, cols] = poolk_ref[:, g, :]
        pool_ref[:, kcols + g * dv:kcols + (g + 1) * dv] = poolv_ref[:, g, :]
    for h in range(heads):
        ahead = (h // hpg) * (dq - LANES)
        keep = slice(ahead, ahead + dq)
        query = queries_ref[h]
        qt_ref[h, keep, :] = query
        empty = slice(dq, span) if ahead == 0 else slice(0, ahead)
        qt_ref[h, empty, :] = jnp.zeros((span - dq, rows), jnp.bfloat16)
        gates[h, :3, :] = jax.nn.sigmoid(mm(gate_ref[h], query))
    count_b = n_seq * blocks
    block_at = lax.broadcasted_iota(jnp.int32, (count_b, rows), 0)
    tile_at = lax.broadcasted_iota(jnp.int32, (1, rows), 1) // BLOCK
    for g in range(groups):
        listed = jnp.full((count_b, rows), NONE, jnp.float32)
        for e in range(list_ref.shape[2]):
            entry = jnp.full((1, rows), -1, jnp.int32)
            for t in range(tiles):
                entry = jnp.where(tile_at == t, list_ref[t, g, e], entry)
            listed = jnp.where(block_at == entry, 0.0, listed)
        bias_ref[g] = listed.reshape(n_seq, blocks, rows)

    def chosen(cost):
        spans = [jnp.max(cost[c:c + 1], axis=1, keepdims=True) for c in range(blocks)]
        there = [jnp.where(top < 0.0, 0.0, 1.0) for top in spans]
        found = []
        for order in (range(blocks), range(blocks - 1, -1, -1)):
            left = jnp.ones_like(there[0])
            share = [None] * blocks
            for c in order:
                share[c] = left * there[c]
                left = left * (1.0 - there[c])
            found.append(share)
        number = sum(there)
        costs = [
            sum(w * cost[c:c + 1] for c, w in enumerate(share))
            + jnp.where(number > need, 0.0, NONE)
            for need, share in zip((0.5, 1.5), found)]
        return found, costs

    def update(h, scores, shift, acc, peak, values, first):
        tall = scores.shape[0]
        if shift is None:
            now = jnp.max(scores, axis=0, keepdims=True)
        else:
            scores = scores.reshape(shift.shape[0], BLOCK, rows)
            now = jnp.max(jnp.max(scores, axis=1) + shift, axis=0, keepdims=True)
        if not first:
            before = peak[h][0:1]
            now = jnp.maximum(before, now)
            shrink = jnp.exp2((before - now) * factor)
        if shift is None:
            raised = jnp.exp2((scores - now) * factor)
        else:
            raised = jnp.exp2((scores + (shift - now)[:, None, :]) * factor).reshape(tall, rows)
        fresh = mm(values, raised.astype(jnp.bfloat16))
        acc[h] = fresh if first else acc[h] * shrink + fresh
        peak[h] = jnp.broadcast_to(now, peak.shape[1:])

    def shard(s, local, window):
        raw = kv[s].astype(jnp.float32).reshape(per, STRIDE, kv.shape[2])
        at = pl.ds(pl.multiple_of(s * per, per), per)
        front[at, :] = jnp.sum(raw * pool_ref[:STRIDE][None], axis=1)
        back[at, :] = jnp.sum(raw * pool_ref[STRIDE:][None], axis=1)
        if window:
            gap = query_at - key_at if local else query_at + rows - key_at
            near[...] = jnp.where((gap >= 0) & (gap < WINDOW), 0.0, NONE)
        for g in range(groups):
            kat = slice(g * LANES, g * LANES + span)
            vat = slice(kcols + g * dv, kcols + (g + 1) * dv)
            if window:
                vt[g, :dv, :] = flip(kv[s, :, vat])
            else:
                found, costs = chosen(bias_ref[g, s])
                for c, (share, cost) in enumerate(zip(found, costs)):
                    few_ref[g, c:c + 1, :] = cost

                    def pick(cols):
                        parts = [
                            kv[s, b * BLOCK:(b + 1) * BLOCK, cols].astype(jnp.float32) * w
                            for b, w in enumerate(share)]
                        return sum(parts[1:], parts[0]).astype(jnp.bfloat16)

                    kfew[g, c * BLOCK:(c + 1) * BLOCK, :] = pick(kat)
                    held_v[c * BLOCK:(c + 1) * BLOCK, :] = pick(vat)
                vfew[g, :dv, :] = flip(held_v[...])

        for g in range(groups):
            kat = slice(g * LANES, g * LANES + span)
            for i in range(hpg):
                h = g * hpg + i
                if window:
                    held_s[i * rows:(i + 1) * rows] = mm(kv[s, :, kat], qt_ref[h])
                else:
                    held_s[i * rows:i * rows + SLOTS * BLOCK] = mm(kfew[g], qt_ref[h])
            for i in range(hpg):
                h = g * hpg + i
                if window:
                    scores = held_s[i * rows:(i + 1) * rows]
                    close = scores + near[...]
                    update(h, close if local else scores, bias_ref[g, s], acc_s, max_s, vt[g], local)
                    update(h, close, None, acc_w, max_w, vt[g], local)
                else:
                    update(h, held_s[i * rows:i * rows + SLOTS * BLOCK], few_ref[g], acc_s, max_s, vfew[g], False)

    shard(me, True, True)

    def step(it, carry):
        d = it // inner
        e = it % inner

        @pl.when((e == 1) & (d < z))
        def _():
            s2 = (z - d - 1) * inner + y
            arrive(s2)
            each_send(s2, 1, lambda copy: copy.start())

        s = (z - d) * inner + (y + e) % inner

        @pl.when((d <= z) & (s < me))
        def _():
            @pl.when(e != 0)
            def _():
                arrive(s)

            @pl.when(s == me - 1)
            def _():
                shard(s, False, True)

            @pl.when(s != me - 1)
            def _():
                shard(s, False, False)

        return carry

    lax.fori_loop(1, n_seq, step, 0)

    count = n_seq * per
    packed = (front[...] + back[pl.ds(1, count), :]).astype(jnp.bfloat16)
    ends = lax.broadcasted_iota(jnp.int32, (count, rows), 0) * STRIDE + (CBLOCK - 1)
    places = me * rows + lax.broadcasted_iota(jnp.int32, (count, rows), 1)
    hidden = jnp.where(ends <= places, 0.0, NONE)
    batch = max(1, min(hpg, held_s.shape[0] // count))
    tail = jnp.ones((ONES, count), jnp.bfloat16)
    for g in range(groups):
        pooled_k = packed[:, g * LANES:g * LANES + span]
        pooled_v = flip(packed[:, kcols + g * dv:kcols + (g + 1) * dv])
        pooled_v = jnp.concatenate([pooled_v, tail], 0)
        for i in range(hpg):
            h = g * hpg + i
            if i % batch == 0:
                for u in range(batch):
                    held_s[u * count:(u + 1) * count] = mm(pooled_k, qt_ref[h + u])
            scores = held_s[i % batch * count:(i % batch + 1) * count] + hidden
            top = jnp.maximum(jnp.max(scores, axis=0, keepdims=True), FLOOR)
            raised = jnp.exp2((scores - top) * factor).astype(jnp.bfloat16)
            branch = mm(pooled_v, raised)
            gate = gates[h]
            total = jnp.zeros((dv, rows), jnp.float32)
            for b, found in enumerate((branch, acc_s[h], acc_w[h])):
                share = gate[b:b + 1] / jnp.maximum(found[dv:dv + 1], 1.0)
                total = total + found[:dv] * share
            mixed[h * dv:(h + 1) * dv, :] = total.astype(jnp.bfloat16)

    weights.wait()
    pieces = outgo.shape[0]
    wide = outgo.shape[1]
    half = pieces * wide

    def swap(j):
        return pltpu.make_async_remote_copy(
            src_ref=outgo.at[j], dst_ref=incoming.at[j], send_sem=psend.at[j],
            recv_sem=precv.at[j], device_id=(part, me, 1 - side), device_id_type=MESH)

    def project(to, j):
        at = pl.ds(pl.multiple_of(to * half + j * wide, wide), wide)
        return mm(w[at, :], mixed[...])

    for j in range(pieces):
        outgo[j] = project(1 - side, j).astype(jnp.bfloat16)
        swap(j).start()
    for j in range(pieces):
        held_p[j] = project(side, j)
    for j in range(pieces):
        swap(j).wait_recv()
        both = held_p[j] + incoming[j].astype(jnp.float32)
        out_ref[:, j * wide:(j + 1) * wide] = jnp.transpose(both).astype(jnp.bfloat16)
    for j in range(pieces):
        swap(j).wait_send()
    each_send(me, 0, lambda copy: copy.wait_send())

    def drain(d, carry):
        @pl.when(d <= z)
        def _():
            each_send((z - d) * inner + y, d, lambda copy: copy.wait_send())

        return carry

    lax.fori_loop(1, outer, drain, 0)


def solution(mesh):
    n_seq = mesh.shape["seq"]
    inner = 2
    while inner * inner * 4 <= n_seq:
        inner *= 2

    def shards(queries, keys, values, lists, gate_weight, pool_key, pool_value, out_weight):
        rows, heads, dq = queries.shape
        groups = keys.shape[1]
        dv = values.shape[2]
        assert groups == 2 and groups * (dq - LANES) == LANES and rows >= WINDOW
        kcols = groups * dq
        kv = jnp.concatenate([keys.reshape(rows, kcols), values.reshape(rows, groups * dv)], 1)
        span = 2 * LANES
        qt = jnp.transpose(queries, (1, 2, 0))
        gw = jnp.transpose(gate_weight, (0, 2, 1))
        blocks = rows // BLOCK
        width = kv.shape[1]
        d_out, d_in = out_weight.shape
        half = d_out // 2
        wide = half // 2
        vmem = pl.BlockSpec(memory_space=pltpu.VMEM)
        hbm = pl.BlockSpec(memory_space=pl.ANY)
        dma = pltpu.SemaphoreType.DMA
        per = rows // STRIDE
        return pl.pallas_call(
            functools.partial(kernel, n_seq, inner, dq ** -0.5 * math.log2(math.e), kcols),
            out_shape=jax.ShapeDtypeStruct((rows, half), jnp.bfloat16),
            in_specs=[hbm, vmem, pl.BlockSpec(memory_space=pltpu.SMEM), vmem, vmem, vmem, hbm],
            out_specs=vmem,
            scratch_shapes=[
                pltpu.VMEM((n_seq, rows, width), jnp.bfloat16),
                pltpu.VMEM((d_out, d_in), jnp.bfloat16),
                pltpu.VMEM((heads, span, rows), jnp.bfloat16),
                pltpu.VMEM((groups, n_seq, blocks, rows), jnp.float32),
                pltpu.VMEM((CBLOCK, width), jnp.float32),
                pltpu.VMEM((heads, dv + ONES, rows), jnp.float32),
                pltpu.VMEM((heads, dv + ONES, rows), jnp.float32),
                pltpu.VMEM((heads, 8, rows), jnp.float32),
                pltpu.VMEM((heads, 8, rows), jnp.float32),
                pltpu.VMEM((groups, dv + ONES, rows), jnp.bfloat16),
                pltpu.VMEM((rows, rows), jnp.float32),
                pltpu.VMEM((n_seq * per, width), jnp.float32),
                pltpu.VMEM((n_seq * per + 8, width), jnp.float32),
                pltpu.VMEM((d_in, rows), jnp.bfloat16),
                pltpu.VMEM((heads, 8, rows), jnp.float32),
                pltpu.VMEM((SLOTS * BLOCK, dv), jnp.bfloat16),
                pltpu.VMEM((groups, SLOTS, rows), jnp.float32),
                pltpu.VMEM((groups, SLOTS * BLOCK, span), jnp.bfloat16),
                pltpu.VMEM((groups, dv + ONES, SLOTS * BLOCK), jnp.bfloat16),
                pltpu.VMEM((half // wide, wide, rows), jnp.bfloat16),
                pltpu.VMEM((half // wide, wide, rows), jnp.bfloat16),
                pltpu.VMEM((max(heads // groups * rows, n_seq * per), rows), jnp.float32),
                pltpu.VMEM((half // wide, wide, rows), jnp.float32),
                dma, dma, dma((n_seq,)), dma((n_seq, inner)), dma((n_seq,)),
                dma((half // wide,)), dma((half // wide,)),
            ],
            compiler_params=pltpu.CompilerParams(
                collective_id=0, has_side_effects=True, vmem_limit_bytes=58 * 1024 * 1024),
        )(kv, qt, lists, gw, pool_key, pool_value, out_weight)

    return jax.shard_map(
        shards,
        mesh=mesh,
        in_specs=(
            P(("groups", "seq"), "head", None),
            P(("groups", "seq"), "head", None),
            P(("groups", "seq"), "head", None),
            P(("groups", "seq"), "head", None),
            P("head", None, None),
            P(None, "head", None),
            P(None, "head", None),
            P(None, "head"),
        ),
        out_specs=P(("groups", "seq"), "head"),
        check_vma=False,
    )
```

```python
import functools
import math

import jax
import jax.numpy as jnp
from jax import lax
from jax.experimental import pallas as pl
from jax.experimental.pallas import tpu as pltpu
from jax.sharding import PartitionSpec as P

BLOCK = 64
CBLOCK = 32
STRIDE = 16
WINDOW = 256
SLOTS = 2
LANES = 128
NONE = -1e30
FLOOR = -1e6
ONES = 16
HALVES = 2
MESH = pl.DeviceIdType.MESH


def mm(a, b):
    return jnp.dot(a, b, preferred_element_type=jnp.float32)


def nt(a, b):
    return lax.dot_general(a, b, (((1,), (1,)), ((), ())), preferred_element_type=jnp.float32)


def kernel(
    n_seq, inner, factor, kcols,
    keys_ref, values_ref, queries_ref, list_ref, gate_ref, poolk_ref, poolv_ref, w_ref, out_ref,
    kv, w, qt_ref, bias_ref, pool_ref, acc_s, acc_w, max_s, max_w, vt, near, front, back, mixed, gates, held_v, few_ref, kfew, vfew,
    outgo, incoming, held_s, held_p, kraw, vraw, eye,
    own_sem, query_sem, w_sem, zsend, ysend, recv, psend, precv,
):
    outer = n_seq // inner
    rows = kv.shape[1]
    heads = qt_ref.shape[0]
    groups = list_ref.shape[1]
    dq = queries_ref.shape[1]
    tiles = list_ref.shape[0]
    hpg = heads // groups
    dv = acc_s.shape[1] - ONES
    span = 2 * LANES
    blocks = rows // BLOCK
    per = rows // STRIDE
    few = SLOTS * BLOCK
    both_ways = inner == 2
    me = lax.axis_index("seq")
    part = lax.axis_index("groups")
    side = lax.axis_index("head")
    z = me // inner
    y = me % inner

    own = [pltpu.make_async_copy(a, b, own_sem.at[i])
           for i, (a, b) in enumerate(((keys_ref, kraw), (values_ref, vraw)))]
    for copy in own:
        copy.start()

    barrier = pltpu.get_barrier_semaphore()

    def greet(who, hd):
        pl.semaphore_signal(barrier, inc=1, device_id=(part, who, hd), device_id_type=MESH)

    greet(me, 1 - side)

    @pl.when(z > 0)
    def _():
        greet(me - inner, side)

    @pl.when(z < outer - 1)
    def _():
        greet(me + inner, side)

    for e in range(1, inner):
        greet(z * inner + (y + e) % inner, side)

    def ahead_of(h):
        return (h // hpg) * (dq - LANES)

    asked = [pltpu.make_async_copy(
        queries_ref.at[g * hpg:(g + 1) * hpg],
        qt_ref.at[g * hpg:(g + 1) * hpg, ahead_of(g * hpg):ahead_of(g * hpg) + dq], query_sem.at[g])
        for g in range(groups)]
    for copy in asked:
        copy.start()
    weights = pltpu.make_async_copy(w_ref, w, w_sem)
    weights.start()

    spot = lax.broadcasted_iota(jnp.int32, (rows, rows), 0)
    eye[...] = jnp.where(spot == lax.broadcasted_iota(jnp.int32, (rows, rows), 1), 1.0, 0.0).astype(jnp.bfloat16)
    from_row = lax.broadcasted_iota(jnp.int32, (rows, rows * groups), 0) * groups
    from_col = lax.broadcasted_iota(jnp.int32, (rows, rows * groups), 1)

    def flip(a):
        n = a.shape[1]
        return nt(eye[:n, :n], a).astype(jnp.bfloat16)

    own[0].wait()
    for g in range(groups):
        kv[me, :, g * dq:(g + 1) * dq] = nt(eye[...], kraw[g * dq:(g + 1) * dq, :]).astype(jnp.bfloat16)
    own[1].wait()
    for g in range(groups):
        pull = jnp.where(from_col == from_row + g, 1.0, 0.0).astype(jnp.bfloat16)
        kv[me, :, kcols + g * dv:kcols + (g + 1) * dv] = mm(pull, vraw[...]).astype(jnp.bfloat16)

    lower = jnp.minimum(z, 1)
    upper = jnp.minimum(outer - 1 - z, 1)
    pl.semaphore_wait(barrier, inner + lower + upper)

    size = rows // HALVES

    def along(s, c):
        return pltpu.make_async_remote_copy(
            src_ref=kv.at[s, c * size:(c + 1) * size], dst_ref=kv.at[s, c * size:(c + 1) * size],
            send_sem=zsend.at[s, c], recv_sem=recv.at[s, c],
            device_id=(part, me + inner, side), device_id_type=MESH)

    def across(s, c, e):
        return pltpu.make_async_remote_copy(
            src_ref=kv.at[s, c * size:(c + 1) * size], dst_ref=kv.at[s, c * size:(c + 1) * size],
            send_sem=ysend.at[s, c, e], recv_sem=recv.at[s, c],
            device_id=(part, z * inner + (y + e) % inner, side), device_id_type=MESH)

    def up(s, c, act):
        @pl.when(z < outer - 1)
        def _():
            act(along(s, c))

    def each_send(s, c, d, act):
        up(s, c, act)
        for e in range(1, inner):
            wanted = (d > 0) | (y + e < inner)
            if both_ways and c == HALVES - 1:
                wanted = (wanted & (d < z)) | (z == 0)

            @pl.when(wanted)
            def _():
                act(across(s, c, e))

    def arrive(s, c):
        pltpu.make_async_remote_copy(
            src_ref=kv.at[s, c * size:(c + 1) * size], dst_ref=kv.at[s, c * size:(c + 1) * size],
            send_sem=zsend.at[s, c], recv_sem=recv.at[s, c],
            device_id=(part, me, 1 - side), device_id_type=MESH).wait_recv()

    def start(copy):
        copy.start()

    def sent(copy):
        copy.wait_send()

    for c in range(HALVES):
        each_send(me, c, 0, start)

    key_at = lax.broadcasted_iota(jnp.int32, (rows, rows), 0)
    query_at = lax.broadcasted_iota(jnp.int32, (rows, rows), 1)
    front[...] = jnp.zeros_like(front)
    back[...] = jnp.zeros_like(back)
    vt[:, dv:, :] = jnp.ones((groups, ONES, rows), jnp.bfloat16)

    vfew[:, dv:, :] = jnp.ones((groups, ONES, vfew.shape[2]), jnp.bfloat16)
    for g in range(groups):
        cols = slice(g * dq, (g + 1) * dq)
        pool_ref[:, cols] = poolk_ref[:, g, :]
        pool_ref[:, kcols + g * dv:kcols + (g + 1) * dv] = poolv_ref[:, g, :]
    for h in range(heads):
        ahead = ahead_of(h)
        empty = slice(dq, span) if ahead == 0 else slice(0, ahead)
        qt_ref[h, empty, :] = jnp.zeros((span - dq, rows), jnp.bfloat16)
    count_b = n_seq * blocks
    block_at = lax.broadcasted_iota(jnp.int32, (count_b, rows), 0)
    tile_at = lax.broadcasted_iota(jnp.int32, (1, rows), 1) // BLOCK
    for g in range(groups):
        listed = jnp.full((count_b, rows), NONE, jnp.float32)
        for e in range(list_ref.shape[2]):
            entry = jnp.full((1, rows), -1, jnp.int32)
            for t in range(tiles):
                entry = jnp.where(tile_at == t, list_ref[t, g, e], entry)
            listed = jnp.where(block_at == entry, 0.0, listed)
        bias_ref[g] = listed.reshape(n_seq, blocks, rows)
    for copy in asked:
        copy.wait()
    gated = gate_ref.shape[0]
    for h in range(heads):
        ahead = ahead_of(h)
        held_s[h * gated:(h + 1) * gated, :] = mm(gate_ref[...], qt_ref[h, ahead:ahead + dq, :])
    for h in range(heads):
        for b in range(gated // heads):
            at = h * gated + b * heads + h
            gates[h, b:b + 1, :] = jax.nn.sigmoid(held_s[at:at + 1, :])

    def chosen(cost):
        spans = [jnp.max(cost[c:c + 1], axis=1, keepdims=True) for c in range(blocks)]
        there = [jnp.where(top < 0.0, 0.0, 1.0) for top in spans]
        found = []
        for order in (range(blocks), range(blocks - 1, -1, -1)):
            left = jnp.ones_like(there[0])
            share = [None] * blocks
            for c in order:
                share[c] = left * there[c]
                left = left * (1.0 - there[c])
            found.append(share)
        number = sum(there)
        costs = [
            sum(w * cost[c:c + 1] for c, w in enumerate(share))
            + jnp.where(number > need, 0.0, NONE)
            for need, share in zip((0.5, 1.5), found)]
        return found, costs

    def update(h, scores, shift, acc, peak, values, first):
        tall = scores.shape[0]
        if shift is None:
            now = jnp.max(scores, axis=0, keepdims=True)
        else:
            scores = scores.reshape(shift.shape[0], BLOCK, rows)
            now = jnp.max(jnp.max(scores, axis=1) + shift, axis=0, keepdims=True)
        if not first:
            before = peak[h][0:1]
            now = jnp.maximum(before, now)
            shrink = jnp.exp2((before - now) * factor)
        if shift is None:
            raised = jnp.exp2((scores - now) * factor)
        else:
            raised = jnp.exp2((scores + (shift - now)[:, None, :]) * factor).reshape(tall, rows)
        fresh = mm(values, raised.astype(jnp.bfloat16))
        acc[h] = fresh if first else acc[h] * shrink + fresh
        peak[h] = jnp.broadcast_to(now, peak.shape[1:])

    def pool(s):
        raw = kv[s].astype(jnp.float32).reshape(per, STRIDE, kv.shape[2])
        at = pl.ds(pl.multiple_of(s * per, per), per)
        front[at, :] = jnp.sum(raw * pool_ref[:STRIDE][None], axis=1)
        back[at, :] = jnp.sum(raw * pool_ref[STRIDE:][None], axis=1)

    def whole(s, local):
        pool(s)
        gap = query_at - key_at if local else query_at + rows - key_at
        near[...] = jnp.where((gap >= 0) & (gap < WINDOW), 0.0, NONE)
        for g in range(groups):
            vt[g, :dv, :] = flip(kv[s, :, kcols + g * dv:kcols + (g + 1) * dv])
        for g in range(groups):
            kat = slice(g * LANES, g * LANES + span)
            for i in range(hpg):
                held_s[i * rows:(i + 1) * rows] = mm(kv[s, :, kat], qt_ref[g * hpg + i])
            for i in range(hpg):
                h = g * hpg + i
                scores = held_s[i * rows:(i + 1) * rows]
                close = scores + near[...]
                update(h, close if local else scores, bias_ref[g, s], acc_s, max_s, vt[g], local)
                update(h, close, None, acc_w, max_w, vt[g], local)

    def take(s, slot):
        pool(s)
        for g in range(groups):
            kat = slice(g * LANES, g * LANES + span)
            vat = slice(kcols + g * dv, kcols + (g + 1) * dv)
            found, costs = chosen(bias_ref[g, s])
            for c, (share, cost) in enumerate(zip(found, costs)):
                few_ref[g, slot * SLOTS + c:slot * SLOTS + c + 1, :] = cost

                def pick(cols):
                    parts = [
                        kv[s, b * BLOCK:(b + 1) * BLOCK, cols].astype(jnp.float32) * w
                        for b, w in enumerate(share)]
                    return sum(parts[1:], parts[0]).astype(jnp.bfloat16)

                kfew[g, slot * few + c * BLOCK:slot * few + (c + 1) * BLOCK, :] = pick(kat)
                held_v[g, c * BLOCK:(c + 1) * BLOCK, :] = pick(vat)
            vfew[g, :dv, slot * few:(slot + 1) * few] = flip(held_v[g])

    def attend(slots):
        tall = slots * few
        for g in range(groups):
            for i in range(hpg):
                held_s[i * rows:i * rows + tall] = mm(kfew[g, :tall], qt_ref[g * hpg + i])
            for i in range(hpg):
                h = g * hpg + i
                update(
                    h, held_s[i * rows:i * rows + tall], few_ref[g, :slots * SLOTS], acc_s, max_s,
                    vfew[g, :, :tall], False)

    whole(me, True)

    def step(k, carry):
        first = 2 * k - 1
        d = first // inner
        e = first % inner
        s1 = (z - d) * inner + (y + e) % inner
        d2 = (first + 1) // inner
        e2 = (first + 1) % inner
        s2 = (z - d2) * inner + (y + e2) % inner

        @pl.when((e == 1) & (d < z))
        def _():
            s3 = (z - d - 1) * inner + y
            for c in range(HALVES):
                arrive(s3, c)
                each_send(s3, c, d + 1, start)

        if both_ways:
            @pl.when(d == z)
            def _():
                arrive(s1, HALVES - 1)
                up(s1, HALVES - 1, start)

        one = (d <= z) & (s1 < me)
        two = (first + 1 < n_seq) & (d2 <= z) & (s2 < me)
        close = one & (s1 == me - 1)
        far = one & (s1 != me - 1)

        @pl.when(one)
        def _():
            for c in range(HALVES - 1):
                arrive(s1, c)
            if both_ways:
                @pl.when(d < z)
                def _():
                    arrive(s1, HALVES - 1)
            else:
                arrive(s1, HALVES - 1)

        @pl.when(two & (e2 != 0))
        def _():
            for c in range(HALVES):
                arrive(s2, c)

        @pl.when(close)
        def _():
            whole(s1, False)

        @pl.when(far & two)
        def _():
            take(s1, 0)
            take(s2, 1)
            attend(2)

        @pl.when(far != two)
        def _():
            take(jnp.where(far, s1, s2), 0)
            attend(1)

        return carry

    lax.fori_loop(1, n_seq // 2 + 1, step, 0)

    count = n_seq * per
    packed = (front[...] + back[pl.ds(1, count), :]).astype(jnp.bfloat16)
    ends = lax.broadcasted_iota(jnp.int32, (count, rows), 0) * STRIDE + (CBLOCK - 1)
    places = me * rows + lax.broadcasted_iota(jnp.int32, (count, rows), 1)
    hidden = jnp.where(ends <= places, 0.0, NONE)
    batch = max(1, min(hpg, held_s.shape[0] // count))
    tail = jnp.ones((ONES, count), jnp.bfloat16)
    for g in range(groups):
        pooled_k = packed[:, g * LANES:g * LANES + span]
        pooled_v = flip(packed[:, kcols + g * dv:kcols + (g + 1) * dv])
        pooled_v = jnp.concatenate([pooled_v, tail], 0)
        for i in range(hpg):
            h = g * hpg + i
            if i % batch == 0:
                for u in range(batch):
                    held_s[u * count:(u + 1) * count] = mm(pooled_k, qt_ref[h + u])
            scores = held_s[i % batch * count:(i % batch + 1) * count] + hidden
            top = jnp.maximum(jnp.max(scores, axis=0, keepdims=True), FLOOR)
            raised = jnp.exp2((scores - top) * factor).astype(jnp.bfloat16)
            branch = mm(pooled_v, raised)
            gate = gates[h]
            total = jnp.zeros((dv, rows), jnp.float32)
            for b, found in enumerate((branch, acc_s[h], acc_w[h])):
                share = gate[b:b + 1] / jnp.maximum(found[dv:dv + 1], 1.0)
                total = total + found[:dv] * share
            mixed[h * dv:(h + 1) * dv, :] = total.astype(jnp.bfloat16)

    weights.wait()
    pieces = outgo.shape[0]
    wide = outgo.shape[1]
    half = pieces * wide

    def swap(j):
        return pltpu.make_async_remote_copy(
            src_ref=outgo.at[j], dst_ref=incoming.at[j], send_sem=psend.at[j],
            recv_sem=precv.at[j], device_id=(part, me, 1 - side), device_id_type=MESH)

    def project(to, j):
        at = pl.ds(pl.multiple_of(to * half + j * wide, wide), wide)
        return mm(w[at, :], mixed[...])

    for j in range(pieces):
        outgo[j] = project(1 - side, j).astype(jnp.bfloat16)
        swap(j).start()
    for j in range(pieces):
        held_p[j] = project(side, j)
    for j in range(pieces):
        swap(j).wait_recv()
        both = held_p[j] + incoming[j].astype(jnp.float32)
        out_ref[:, j * wide:(j + 1) * wide] = jnp.transpose(both).astype(jnp.bfloat16)
    for j in range(pieces):
        swap(j).wait_send()
    for c in range(HALVES):
        each_send(me, c, 0, sent)

    def drain(d, carry):
        @pl.when(d <= z)
        def _():
            for c in range(HALVES):
                each_send((z - d) * inner + y, c, d, sent)

        return carry

    lax.fori_loop(1, outer, drain, 0)
    if both_ways:
        up(1 - y, HALVES - 1, sent)


def solution(mesh):
    n_seq = mesh.shape["seq"]
    inner = 2
    while inner * inner * 4 <= n_seq:
        inner *= 2

    def shards(queries, keys, values, lists, gate_weight, pool_key, pool_value, out_weight):
        rows, heads, dq = queries.shape
        groups = keys.shape[1]
        dv = values.shape[2]
        assert groups == 2 and groups * (dq - LANES) == LANES and rows >= WINDOW
        kcols = groups * dq
        kt = jnp.transpose(keys, (1, 2, 0)).reshape(kcols, rows)
        flat = values.reshape(rows * groups, dv)
        span = 2 * LANES
        qt = jnp.transpose(queries, (1, 2, 0))
        gw = jnp.transpose(gate_weight, (2, 0, 1)).reshape(-1, dq)
        blocks = rows // BLOCK
        width = kcols + groups * dv
        d_out, d_in = out_weight.shape
        half = d_out // 2
        wide = half // 2
        vmem = pl.BlockSpec(memory_space=pltpu.VMEM)
        hbm = pl.BlockSpec(memory_space=pl.ANY)
        dma = pltpu.SemaphoreType.DMA
        per = rows // STRIDE
        return pl.pallas_call(
            functools.partial(kernel, n_seq, inner, dq ** -0.5 * math.log2(math.e), kcols),
            out_shape=jax.ShapeDtypeStruct((rows, half), jnp.bfloat16),
            in_specs=[hbm, hbm, hbm, pl.BlockSpec(memory_space=pltpu.SMEM), vmem, vmem, vmem, hbm],
            out_specs=vmem,
            scratch_shapes=[
                pltpu.VMEM((n_seq, rows, width), jnp.bfloat16),
                pltpu.VMEM((d_out, d_in), jnp.bfloat16),
                pltpu.VMEM((heads, span, rows), jnp.bfloat16),
                pltpu.VMEM((groups, n_seq, blocks, rows), jnp.float32),
                pltpu.VMEM((CBLOCK, width), jnp.float32),
                pltpu.VMEM((heads, dv + ONES, rows), jnp.float32),
                pltpu.VMEM((heads, dv + ONES, rows), jnp.float32),
                pltpu.VMEM((heads, 8, rows), jnp.float32),
                pltpu.VMEM((heads, 8, rows), jnp.float32),
                pltpu.VMEM((groups, dv + ONES, rows), jnp.bfloat16),
                pltpu.VMEM((rows, rows), jnp.float32),
                pltpu.VMEM((n_seq * per, width), jnp.float32),
                pltpu.VMEM((n_seq * per + 8, width), jnp.float32),
                pltpu.VMEM((d_in, rows), jnp.bfloat16),
                pltpu.VMEM((heads, 8, rows), jnp.float32),
                pltpu.VMEM((groups, SLOTS * BLOCK, dv), jnp.bfloat16),
                pltpu.VMEM((groups, 2 * SLOTS, rows), jnp.float32),
                pltpu.VMEM((groups, 2 * SLOTS * BLOCK, span), jnp.bfloat16),
                pltpu.VMEM((groups, dv + ONES, 2 * SLOTS * BLOCK), jnp.bfloat16),
                pltpu.VMEM((half // wide, wide, rows), jnp.bfloat16),
                pltpu.VMEM((half // wide, wide, rows), jnp.bfloat16),
                pltpu.VMEM((max(heads // groups * rows, n_seq * per), rows), jnp.float32),
                pltpu.VMEM((half // wide, wide, rows), jnp.float32),
                pltpu.VMEM((kcols, rows), jnp.bfloat16),
                pltpu.VMEM((rows * groups, dv), jnp.bfloat16),
                pltpu.VMEM((rows, rows), jnp.bfloat16),
                dma((2,)), dma((groups,)), dma, dma((n_seq, HALVES)), dma((n_seq, HALVES, inner)), dma((n_seq, HALVES)),
                dma((half // wide,)), dma((half // wide,)),
            ],
            compiler_params=pltpu.CompilerParams(
                collective_id=0, has_side_effects=True, vmem_limit_bytes=58 * 1024 * 1024),
        )(kt, flat, qt, lists, gw, pool_key, pool_value, out_weight)

    return jax.shard_map(
        shards,
        mesh=mesh,
        in_specs=(
            P(("groups", "seq"), "head", None),
            P(("groups", "seq"), "head", None),
            P(("groups", "seq"), "head", None),
            P(("groups", "seq"), "head", None),
            P("head", None, None),
            P(None, "head", None),
            P(None, "head", None),
            P(None, "head"),
        ),
        out_specs=P(("groups", "seq"), "head"),
        check_vma=False,
    )
```

```python
import functools
import math

import jax
import jax.numpy as jnp
from jax import lax
from jax.experimental import pallas as pl
from jax.experimental.pallas import tpu as pltpu
from jax.sharding import PartitionSpec as P

BLOCK = 64
CBLOCK = 32
STRIDE = 16
WINDOW = 256
SLOTS = 2
LANES = 128
NONE = -1e30
FLOOR = -1e6
ONES = 16
HALVES = 2
MESH = pl.DeviceIdType.MESH


def mm(a, b):
    return jnp.dot(a, b, preferred_element_type=jnp.float32)


def nt(a, b):
    return lax.dot_general(a, b, (((1,), (1,)), ((), ())), preferred_element_type=jnp.float32)


def kernel(
    n_seq, inner, factor, kcols,
    keys_ref, values_ref, queries_ref, lists_ref, gates_ref, poolks_ref, poolvs_ref, w_ref, out_ref,
    kv, w, qt_ref, bias_ref, pool_ref, acc_s, acc_w, max_s, max_w, vt, near, front, back, mixed, gates, held_v, few_ref, kfew, vfew,
    outgo, incoming, held_s, held_p, kraw, vraw, eye, acc_c, max_c,
    list_ref, gate_ref, poolk_ref, poolv_ref,
    own_sem, small_sem, query_sem, w_sem, zsend, ysend, recv, psend, precv,
):
    outer = n_seq // inner
    rows = kv.shape[1]
    heads = qt_ref.shape[0]
    groups = list_ref.shape[1]
    dq = queries_ref.shape[1]
    tiles = list_ref.shape[0]
    hpg = heads // groups
    dv = acc_s.shape[1] - ONES
    span = 2 * LANES
    blocks = rows // BLOCK
    per = rows // STRIDE
    few = SLOTS * BLOCK
    both_ways = inner == 2
    me = lax.axis_index("seq")
    part = lax.axis_index("groups")
    side = lax.axis_index("head")
    z = me // inner
    y = me % inner

    own = [pltpu.make_async_copy(a, b, own_sem.at[i])
           for i, (a, b) in enumerate(((keys_ref, kraw), (values_ref, vraw)))]
    for copy in own:
        copy.start()

    barrier = pltpu.get_barrier_semaphore()

    def greet(who, hd):
        pl.semaphore_signal(barrier, inc=1, device_id=(part, who, hd), device_id_type=MESH)

    greet(me, 1 - side)

    @pl.when(z > 0)
    def _():
        greet(me - inner, side)

    @pl.when(z < outer - 1)
    def _():
        greet(me + inner, side)

    for e in range(1, inner):
        greet(z * inner + (y + e) % inner, side)

    def ahead_of(h):
        return (h // hpg) * (dq - LANES)

    small = [pltpu.make_async_copy(a, b, small_sem.at[i]) for i, (a, b) in enumerate((
        (lists_ref, list_ref), (gates_ref, gate_ref), (poolks_ref, poolk_ref), (poolvs_ref, poolv_ref)))]
    for copy in small:
        copy.start()
    asked = [pltpu.make_async_copy(
        queries_ref.at[g * hpg:(g + 1) * hpg],
        qt_ref.at[g * hpg:(g + 1) * hpg, ahead_of(g * hpg):ahead_of(g * hpg) + dq], query_sem.at[g])
        for g in range(groups)]
    for copy in asked:
        copy.start()
    weights = pltpu.make_async_copy(w_ref, w, w_sem)
    weights.start()

    spot = lax.broadcasted_iota(jnp.int32, (rows, rows), 0)
    eye[...] = jnp.where(spot == lax.broadcasted_iota(jnp.int32, (rows, rows), 1), 1.0, 0.0).astype(jnp.bfloat16)
    from_row = lax.broadcasted_iota(jnp.int32, (rows, rows * groups), 0) * groups
    from_col = lax.broadcasted_iota(jnp.int32, (rows, rows * groups), 1)

    def flip(a):
        n = a.shape[1]
        return nt(eye[:n, :n], a).astype(jnp.bfloat16)

    own[0].wait()
    for g in range(groups):
        kv[me, :, g * dq:(g + 1) * dq] = nt(eye[...], kraw[g * dq:(g + 1) * dq, :]).astype(jnp.bfloat16)
    own[1].wait()
    for g in range(groups):
        pull = jnp.where(from_col == from_row + g, 1.0, 0.0).astype(jnp.bfloat16)
        kv[me, :, kcols + g * dv:kcols + (g + 1) * dv] = mm(pull, vraw[...]).astype(jnp.bfloat16)

    lower = jnp.minimum(z, 1)
    upper = jnp.minimum(outer - 1 - z, 1)
    pl.semaphore_wait(barrier, inner + lower + upper)

    size = rows // HALVES

    def along(s, c):
        return pltpu.make_async_remote_copy(
            src_ref=kv.at[s, c * size:(c + 1) * size], dst_ref=kv.at[s, c * size:(c + 1) * size],
            send_sem=zsend.at[s, c], recv_sem=recv.at[s, c],
            device_id=(part, me + inner, side), device_id_type=MESH)

    def across(s, c, e):
        return pltpu.make_async_remote_copy(
            src_ref=kv.at[s, c * size:(c + 1) * size], dst_ref=kv.at[s, c * size:(c + 1) * size],
            send_sem=ysend.at[s, c, e], recv_sem=recv.at[s, c],
            device_id=(part, z * inner + (y + e) % inner, side), device_id_type=MESH)

    def up(s, c, act):
        @pl.when(z < outer - 1)
        def _():
            act(along(s, c))

    def each_send(s, c, d, act):
        up(s, c, act)
        for e in range(1, inner):
            wanted = (d > 0) | (y + e < inner)
            if both_ways and c == HALVES - 1:
                wanted = (wanted & (d < z)) | (z == 0)

            @pl.when(wanted)
            def _():
                act(across(s, c, e))

    def arrive(s, c):
        pltpu.make_async_remote_copy(
            src_ref=kv.at[s, c * size:(c + 1) * size], dst_ref=kv.at[s, c * size:(c + 1) * size],
            send_sem=zsend.at[s, c], recv_sem=recv.at[s, c],
            device_id=(part, me, 1 - side), device_id_type=MESH).wait_recv()

    def start(copy):
        copy.start()

    def sent(copy):
        copy.wait_send()

    for c in range(HALVES):
        each_send(me, c, 0, start)

    key_at = lax.broadcasted_iota(jnp.int32, (rows, rows), 0)
    query_at = lax.broadcasted_iota(jnp.int32, (rows, rows), 1)
    front[...] = jnp.zeros_like(front)
    back[...] = jnp.zeros_like(back)
    vt[:, dv:, :] = jnp.ones((groups, ONES, rows), jnp.bfloat16)

    vfew[:, dv:, :] = jnp.ones((groups, ONES, vfew.shape[2]), jnp.bfloat16)
    for copy in small:
        copy.wait()
    for g in range(groups):
        cols = slice(g * dq, (g + 1) * dq)
        pool_ref[:, cols] = poolk_ref[:, g, :]
        pool_ref[:, kcols + g * dv:kcols + (g + 1) * dv] = poolv_ref[:, g, :]
    for h in range(heads):
        ahead = ahead_of(h)
        empty = slice(dq, span) if ahead == 0 else slice(0, ahead)
        qt_ref[h, empty, :] = jnp.zeros((span - dq, rows), jnp.bfloat16)
    count_b = n_seq * blocks
    block_at = lax.broadcasted_iota(jnp.int32, (count_b, rows), 0)
    tile_at = lax.broadcasted_iota(jnp.int32, (1, rows), 1) // BLOCK
    for g in range(groups):
        listed = jnp.full((count_b, rows), NONE, jnp.float32)
        for e in range(list_ref.shape[2]):
            entry = jnp.full((1, rows), -1, jnp.int32)
            for t in range(tiles):
                entry = jnp.where(tile_at == t, list_ref[t, g, e], entry)
            listed = jnp.where(block_at == entry, 0.0, listed)
        bias_ref[g] = listed.reshape(n_seq, blocks, rows)
    for copy in asked:
        copy.wait()
    gated = gate_ref.shape[0]
    for h in range(heads):
        ahead = ahead_of(h)
        held_s[h * gated:(h + 1) * gated, :] = mm(gate_ref[...], qt_ref[h, ahead:ahead + dq, :])
    for h in range(heads):
        for b in range(gated // heads):
            at = h * gated + b * heads + h
            gates[h, b:b + 1, :] = jax.nn.sigmoid(held_s[at:at + 1, :])

    def chosen(cost):
        spans = [jnp.max(cost[c:c + 1], axis=1, keepdims=True) for c in range(blocks)]
        there = [jnp.where(top < 0.0, 0.0, 1.0) for top in spans]
        found = []
        for order in (range(blocks), range(blocks - 1, -1, -1)):
            left = jnp.ones_like(there[0])
            share = [None] * blocks
            for c in order:
                share[c] = left * there[c]
                left = left * (1.0 - there[c])
            found.append(share)
        number = sum(there)
        costs = [
            sum(w * cost[c:c + 1] for c, w in enumerate(share))
            + jnp.where(number > need, 0.0, NONE)
            for need, share in zip((0.5, 1.5), found)]
        return found, costs

    def update(h, scores, shift, acc, peak, values, first):
        tall = scores.shape[0]
        if shift is None:
            now = jnp.max(scores, axis=0, keepdims=True)
        else:
            scores = scores.reshape(shift.shape[0], BLOCK, rows)
            now = jnp.max(jnp.max(scores, axis=1) + shift, axis=0, keepdims=True)
        if not first:
            before = peak[h][0:1]
            now = jnp.maximum(before, now)
            shrink = jnp.exp2((before - now) * factor)
        if shift is None:
            raised = jnp.exp2((scores - now) * factor)
        else:
            raised = jnp.exp2((scores + (shift - now)[:, None, :]) * factor).reshape(tall, rows)
        fresh = mm(values, raised.astype(jnp.bfloat16))
        acc[h] = fresh if first else acc[h] * shrink + fresh
        peak[h] = jnp.broadcast_to(now, peak.shape[1:])

    def pool(s):
        raw = kv[s].astype(jnp.float32).reshape(per, STRIDE, kv.shape[2])
        at = pl.ds(pl.multiple_of(s * per, per), per)
        front[at, :] = jnp.sum(raw * pool_ref[:STRIDE][None], axis=1)
        back[at, :] = jnp.sum(raw * pool_ref[STRIDE:][None], axis=1)

    def whole(s, local):
        pool(s)
        gap = query_at - key_at if local else query_at + rows - key_at
        near[...] = jnp.where((gap >= 0) & (gap < WINDOW), 0.0, NONE)
        for g in range(groups):
            vt[g, :dv, :] = flip(kv[s, :, kcols + g * dv:kcols + (g + 1) * dv])
        for g in range(groups):
            kat = slice(g * LANES, g * LANES + span)
            for i in range(hpg):
                held_s[i * rows:(i + 1) * rows] = mm(kv[s, :, kat], qt_ref[g * hpg + i])
            for i in range(hpg):
                h = g * hpg + i
                scores = held_s[i * rows:(i + 1) * rows]
                close = scores + near[...]
                update(h, close if local else scores, bias_ref[g, s], acc_s, max_s, vt[g], local)
                update(h, close, None, acc_w, max_w, vt[g], local)

    def take(s, slot):
        pool(s)
        for g in range(groups):
            kat = slice(g * LANES, g * LANES + span)
            vat = slice(kcols + g * dv, kcols + (g + 1) * dv)
            found, costs = chosen(bias_ref[g, s])
            for c, (share, cost) in enumerate(zip(found, costs)):
                few_ref[g, slot * SLOTS + c:slot * SLOTS + c + 1, :] = cost

                def pick(cols):
                    parts = [
                        kv[s, b * BLOCK:(b + 1) * BLOCK, cols].astype(jnp.float32) * w
                        for b, w in enumerate(share)]
                    return sum(parts[1:], parts[0]).astype(jnp.bfloat16)

                kfew[g, slot * few + c * BLOCK:slot * few + (c + 1) * BLOCK, :] = pick(kat)
                held_v[g, c * BLOCK:(c + 1) * BLOCK, :] = pick(vat)
            vfew[g, :dv, slot * few:(slot + 1) * few] = flip(held_v[g])

    def attend(slots):
        tall = slots * few
        for g in range(groups):
            for i in range(hpg):
                held_s[i * rows:i * rows + tall] = mm(kfew[g, :tall], qt_ref[g * hpg + i])
            for i in range(hpg):
                h = g * hpg + i
                update(
                    h, held_s[i * rows:i * rows + tall], few_ref[g, :slots * SLOTS], acc_s, max_s,
                    vfew[g, :, :tall], False)

    whole(me, True)

    def step(k, carry):
        first = 2 * k - 1
        d = first // inner
        e = first % inner
        s1 = (z - d) * inner + (y + e) % inner
        d2 = (first + 1) // inner
        e2 = (first + 1) % inner
        s2 = (z - d2) * inner + (y + e2) % inner

        @pl.when((e == 1) & (d < z))
        def _():
            s3 = (z - d - 1) * inner + y
            for c in range(HALVES):
                arrive(s3, c)
                each_send(s3, c, d + 1, start)

        one = (d <= z) & (s1 < me)
        two = (first + 1 < n_seq) & (d2 <= z) & (s2 < me)
        close = one & (s1 == me - 1)
        far = one & (s1 != me - 1)

        @pl.when(one)
        def _():
            for c in range(HALVES):
                arrive(s1, c)

        @pl.when(two & (e2 != 0))
        def _():
            for c in range(HALVES):
                arrive(s2, c)

        @pl.when(close)
        def _():
            whole(s1, False)

        @pl.when(far & two)
        def _():
            take(s1, 0)
            take(s2, 1)
            attend(2)

        @pl.when(far != two)
        def _():
            take(jnp.where(far, s1, s2), 0)
            attend(1)

        return carry

    count = n_seq * per
    late = 2 * per
    last = 1 - y
    places = me * rows + lax.broadcasted_iota(jnp.int32, (1, rows), 1)
    tail = jnp.ones((ONES, count), jnp.bfloat16)
    batch = max(1, min(hpg, held_s.shape[0] // count))

    def hide(number, of_last):
        token = lax.broadcasted_iota(jnp.int32, (number, rows), 0)
        seen = token * STRIDE + (CBLOCK - 1) <= places
        if both_ways:
            touched = (token >= last * per - 1) & (token < (last + 1) * per)
            seen = seen & (touched if of_last else jnp.logical_not(touched))
        return jnp.where(seen, 0.0, NONE)

    def compressed():
        packed = (front[...] + back[pl.ds(1, count), :]).astype(jnp.bfloat16)
        hidden = hide(count, False)
        for g in range(groups):
            pooled_k = packed[:, g * LANES:g * LANES + span]
            pooled_v = flip(packed[:, kcols + g * dv:kcols + (g + 1) * dv])
            pooled_v = jnp.concatenate([pooled_v, tail], 0)
            for i in range(hpg):
                h = g * hpg + i
                if i % batch == 0:
                    for u in range(batch):
                        held_s[u * count:(u + 1) * count] = mm(pooled_k, qt_ref[h + u])
                scores = held_s[i % batch * count:(i % batch + 1) * count] + hidden
                top = jnp.maximum(jnp.max(scores, axis=0, keepdims=True), FLOOR)
                raised = jnp.exp2((scores - top) * factor).astype(jnp.bfloat16)
                acc_c[h] = mm(pooled_v, raised)
                max_c[h] = jnp.broadcast_to(top, max_c.shape[1:])

    def rest(tall):
        packed = (front[:late] + back[1:late + 1]).astype(jnp.bfloat16)
        hidden = hide(late, True)
        for g in range(groups):
            kfew[g, few:few + late, :] = packed[:, g * LANES:g * LANES + span]
            vfew[g, :dv, few:few + late] = flip(packed[:, kcols + g * dv:kcols + (g + 1) * dv])
        for g in range(groups):
            for i in range(hpg):
                held_s[i * rows:i * rows + tall + late] = mm(kfew[g, few - tall:few + late], qt_ref[g * hpg + i])
            for i in range(hpg):
                h = g * hpg + i
                if tall:
                    update(
                        h, held_s[i * rows:i * rows + tall], few_ref[g, :SLOTS], acc_s, max_s,
                        vfew[g, :, :tall], False)
                update(
                    h, held_s[i * rows + tall:i * rows + tall + late] + hidden, None, acc_c, max_c,
                    vfew[g, :, few:few + late], False)

    if both_ways:
        lax.fori_loop(1, z + 1, step, 0)
        compressed()
        arrive(last, HALVES - 1)
        up(last, HALVES - 1, start)

        @pl.when(me > 0)
        def _():
            for c in range(HALVES - 1):
                arrive(last, c)

        @pl.when((me > 0) & (last == me - 1))
        def _():
            whole(last, False)
            rest(0)

        @pl.when((me > 0) & (last != me - 1))
        def _():
            take(last, 0)
            rest(few)
    else:
        lax.fori_loop(1, n_seq // 2 + 1, step, 0)
        compressed()

    for h in range(heads):
        gate = gates[h]
        total = jnp.zeros((dv, rows), jnp.float32)
        for b, found in enumerate((acc_c[h], acc_s[h], acc_w[h])):
            share = gate[b:b + 1] / jnp.maximum(found[dv:dv + 1], 1.0)
            total = total + found[:dv] * share
        mixed[h * dv:(h + 1) * dv, :] = total.astype(jnp.bfloat16)

    weights.wait()
    pieces = outgo.shape[0]
    wide = outgo.shape[1]
    half = pieces * wide

    def swap(j):
        return pltpu.make_async_remote_copy(
            src_ref=outgo.at[j], dst_ref=incoming.at[j], send_sem=psend.at[j],
            recv_sem=precv.at[j], device_id=(part, me, 1 - side), device_id_type=MESH)

    def project(to, j):
        at = pl.ds(pl.multiple_of(to * half + j * wide, wide), wide)
        return mm(w[at, :], mixed[...])

    for j in range(pieces):
        outgo[j] = project(1 - side, j).astype(jnp.bfloat16)
        swap(j).start()
    def finish(j):
        both = held_p[j] + incoming[j].astype(jnp.float32)
        out_ref[:, j * wide:(j + 1) * wide] = jnp.transpose(both).astype(jnp.bfloat16)

    for j in range(pieces):
        held_p[j] = project(side, j)
    for j in range(pieces):
        swap(j).wait_recv()
        finish(j)
    for j in range(pieces):
        swap(j).wait_send()
    for c in range(HALVES):
        each_send(me, c, 0, sent)

    def drain(d, carry):
        @pl.when(d <= z)
        def _():
            for c in range(HALVES):
                each_send((z - d) * inner + y, c, d, sent)

        return carry

    lax.fori_loop(1, outer, drain, 0)
    if both_ways:
        up(1 - y, HALVES - 1, sent)


def solution(mesh):
    n_seq = mesh.shape["seq"]
    inner = 2
    while inner * inner * 4 <= n_seq:
        inner *= 2

    def shards(queries, keys, values, lists, gate_weight, pool_key, pool_value, out_weight):
        rows, heads, dq = queries.shape
        groups = keys.shape[1]
        dv = values.shape[2]
        assert groups == 2 and groups * (dq - LANES) == LANES and rows >= WINDOW
        kcols = groups * dq
        kt = jnp.transpose(keys, (1, 2, 0)).reshape(kcols, rows)
        flat = values.reshape(rows * groups, dv)
        span = 2 * LANES
        qt = jnp.transpose(queries, (1, 2, 0))
        gw = jnp.transpose(gate_weight, (2, 0, 1)).reshape(-1, dq)
        blocks = rows // BLOCK
        width = kcols + groups * dv
        d_out, d_in = out_weight.shape
        half = d_out // 2
        wide = half // 2
        vmem = pl.BlockSpec(memory_space=pltpu.VMEM)
        hbm = pl.BlockSpec(memory_space=pltpu.HBM)
        dma = pltpu.SemaphoreType.DMA
        per = rows // STRIDE
        return pl.pallas_call(
            functools.partial(kernel, n_seq, inner, dq ** -0.5 * math.log2(math.e), kcols),
            out_shape=jax.ShapeDtypeStruct((rows, half), jnp.bfloat16),
            in_specs=[hbm] * 8,
            out_specs=vmem,
            scratch_shapes=[
                pltpu.VMEM((n_seq, rows, width), jnp.bfloat16),
                pltpu.VMEM((d_out, d_in), jnp.bfloat16),
                pltpu.VMEM((heads, span, rows), jnp.bfloat16),
                pltpu.VMEM((groups, n_seq, blocks, rows), jnp.float32),
                pltpu.VMEM((CBLOCK, width), jnp.float32),
                pltpu.VMEM((heads, dv + ONES, rows), jnp.float32),
                pltpu.VMEM((heads, dv + ONES, rows), jnp.float32),
                pltpu.VMEM((heads, 8, rows), jnp.float32),
                pltpu.VMEM((heads, 8, rows), jnp.float32),
                pltpu.VMEM((groups, dv + ONES, rows), jnp.bfloat16),
                pltpu.VMEM((rows, rows), jnp.float32),
                pltpu.VMEM((n_seq * per, width), jnp.float32),
                pltpu.VMEM((n_seq * per + 8, width), jnp.float32),
                pltpu.VMEM((d_in, rows), jnp.bfloat16),
                pltpu.VMEM((heads, 8, rows), jnp.float32),
                pltpu.VMEM((groups, SLOTS * BLOCK, dv), jnp.bfloat16),
                pltpu.VMEM((groups, 2 * SLOTS, rows), jnp.float32),
                pltpu.VMEM((groups, 2 * SLOTS * BLOCK, span), jnp.bfloat16),
                pltpu.VMEM((groups, dv + ONES, 2 * SLOTS * BLOCK), jnp.bfloat16),
                pltpu.VMEM((half // wide, wide, rows), jnp.bfloat16),
                pltpu.VMEM((half // wide, wide, rows), jnp.bfloat16),
                pltpu.VMEM((max(heads // groups * rows, n_seq * per), rows), jnp.float32),
                pltpu.VMEM((half // wide, wide, rows), jnp.float32),
                pltpu.VMEM((kcols, rows), jnp.bfloat16),
                pltpu.VMEM((rows * groups, dv), jnp.bfloat16),
                pltpu.VMEM((rows, rows), jnp.bfloat16),
                pltpu.VMEM((heads, dv + ONES, rows), jnp.float32),
                pltpu.VMEM((heads, 8, rows), jnp.float32),
                pltpu.SMEM(lists.shape, jnp.int32),
                pltpu.VMEM(gw.shape, jnp.bfloat16),
                pltpu.VMEM(pool_key.shape, jnp.float32),
                pltpu.VMEM(pool_value.shape, jnp.float32),
                dma((2,)), dma((4,)), dma((groups,)), dma, dma((n_seq, HALVES)), dma((n_seq, HALVES, inner)), dma((n_seq, HALVES)),
                dma((half // wide,)), dma((half // wide,)),
            ],
            compiler_params=pltpu.CompilerParams(
                collective_id=0, has_side_effects=True, vmem_limit_bytes=(50 if n_seq <= 8 else 61) * 1024 * 1024),
        )(*(pltpu.with_memory_space_constraint(a, pltpu.HBM) for a in (kt, flat, qt, lists, gw, pool_key, pool_value, out_weight)))

    return jax.shard_map(
        shards,
        mesh=mesh,
        in_specs=(
            P(("groups", "seq"), "head", None),
            P(("groups", "seq"), "head", None),
            P(("groups", "seq"), "head", None),
            P(("groups", "seq"), "head", None),
            P("head", None, None),
            P(None, "head", None),
            P(None, "head", None),
            P(None, "head"),
        ),
        out_specs=P(("groups", "seq"), "head"),
        check_vma=False,
    )
```

```python
import functools
import math

import jax
import jax.numpy as jnp
from jax import lax
from jax.experimental import pallas as pl
from jax.experimental.pallas import tpu as pltpu
from jax.sharding import PartitionSpec as P

BLOCK = 64
CBLOCK = 32
STRIDE = 16
WINDOW = 256
SLOTS = 2
LANES = 128
NONE = -1e30
FLOOR = -1e6
ONES = 16
HALVES = 2
MESH = pl.DeviceIdType.MESH


def mm(a, b):
    return jnp.dot(a, b, preferred_element_type=jnp.float32)


def nt(a, b):
    return lax.dot_general(a, b, (((1,), (1,)), ((), ())), preferred_element_type=jnp.float32)


def kernel(
    n_seq, inner, factor, kcols,
    keys_ref, values_ref, queries_ref, lists_ref, gates_ref, poolks_ref, poolvs_ref, w_ref, out_ref,
    kv, w, qt_ref, bias_ref, pool_ref, acc_s, acc_w, max_s, max_w, vt, near, front, back, mixed, gates, held_v, few_ref, kfew, vfew,
    outgo, incoming, held_s, held_p, kraw, vraw, eye, acc_c, max_c,
    list_ref, gate_ref, poolk_ref, poolv_ref,
    own_sem, small_sem, query_sem, w_sem, zsend, ysend, recv, psend, precv,
):
    outer = n_seq // inner
    rows = kv.shape[1]
    heads = qt_ref.shape[0]
    groups = list_ref.shape[1]
    dq = queries_ref.shape[1]
    tiles = list_ref.shape[0]
    hpg = heads // groups
    dv = acc_s.shape[1] - ONES
    span = 2 * LANES
    blocks = rows // BLOCK
    per = rows // STRIDE
    few = SLOTS * BLOCK
    both_ways = inner == 2
    me = lax.axis_index("seq")
    part = lax.axis_index("groups")
    side = lax.axis_index("head")
    z = me // inner
    y = me % inner

    own = [pltpu.make_async_copy(a, b, own_sem.at[i])
           for i, (a, b) in enumerate(((keys_ref, kraw), (values_ref, vraw)))]
    for copy in own:
        copy.start()

    barrier = pltpu.get_barrier_semaphore()

    def greet(who, hd):
        pl.semaphore_signal(barrier, inc=1, device_id=(part, who, hd), device_id_type=MESH)

    greet(me, 1 - side)

    @pl.when(z > 0)
    def _():
        greet(me - inner, side)

    @pl.when(z < outer - 1)
    def _():
        greet(me + inner, side)

    for e in range(1, inner):
        greet(z * inner + (y + e) % inner, side)

    def ahead_of(h):
        return (h // hpg) * (dq - LANES)

    small = [pltpu.make_async_copy(a, b, small_sem.at[i]) for i, (a, b) in enumerate((
        (lists_ref, list_ref), (gates_ref, gate_ref), (poolks_ref, poolk_ref), (poolvs_ref, poolv_ref)))]
    for copy in small:
        copy.start()
    asked = [pltpu.make_async_copy(
        queries_ref.at[g * hpg:(g + 1) * hpg],
        qt_ref.at[g * hpg:(g + 1) * hpg, ahead_of(g * hpg):ahead_of(g * hpg) + dq], query_sem.at[g])
        for g in range(groups)]
    for copy in asked:
        copy.start()
    weights = pltpu.make_async_copy(w_ref, w, w_sem)
    weights.start()

    spot = lax.broadcasted_iota(jnp.int32, (rows, rows), 0)
    eye[...] = jnp.where(spot == lax.broadcasted_iota(jnp.int32, (rows, rows), 1), 1.0, 0.0).astype(jnp.bfloat16)
    from_row = lax.broadcasted_iota(jnp.int32, (rows, rows * groups), 0) * groups
    from_col = lax.broadcasted_iota(jnp.int32, (rows, rows * groups), 1)

    def flip(a):
        n = a.shape[1]
        return nt(eye[:n, :n], a).astype(jnp.bfloat16)

    own[0].wait()
    for g in range(groups):
        kv[me, :, g * dq:(g + 1) * dq] = nt(eye[...], kraw[g * dq:(g + 1) * dq, :]).astype(jnp.bfloat16)
    own[1].wait()
    for g in range(groups):
        pull = jnp.where(from_col == from_row + g, 1.0, 0.0).astype(jnp.bfloat16)
        kv[me, :, kcols + g * dv:kcols + (g + 1) * dv] = mm(pull, vraw[...]).astype(jnp.bfloat16)

    lower = jnp.minimum(z, 1)
    upper = jnp.minimum(outer - 1 - z, 1)
    pl.semaphore_wait(barrier, inner + lower + upper)

    size = rows // HALVES

    def along(s, c):
        return pltpu.make_async_remote_copy(
            src_ref=kv.at[s, c * size:(c + 1) * size], dst_ref=kv.at[s, c * size:(c + 1) * size],
            send_sem=zsend.at[s, c], recv_sem=recv.at[s, c],
            device_id=(part, me + inner, side), device_id_type=MESH)

    def across(s, c, e):
        return pltpu.make_async_remote_copy(
            src_ref=kv.at[s, c * size:(c + 1) * size], dst_ref=kv.at[s, c * size:(c + 1) * size],
            send_sem=ysend.at[s, c, e], recv_sem=recv.at[s, c],
            device_id=(part, z * inner + (y + e) % inner, side), device_id_type=MESH)

    def up(s, c, act):
        @pl.when(z < outer - 1)
        def _():
            act(along(s, c))

    def each_send(s, c, d, act):
        up(s, c, act)
        for e in range(1, inner):
            wanted = (d > 0) | (y + e < inner)
            if both_ways and c == HALVES - 1:
                wanted = (wanted & (d < z)) | (z == 0)

            @pl.when(wanted)
            def _():
                act(across(s, c, e))

    def arrive(s, c):
        pltpu.make_async_remote_copy(
            src_ref=kv.at[s, c * size:(c + 1) * size], dst_ref=kv.at[s, c * size:(c + 1) * size],
            send_sem=zsend.at[s, c], recv_sem=recv.at[s, c],
            device_id=(part, me, 1 - side), device_id_type=MESH).wait_recv()

    def start(copy):
        copy.start()

    def sent(copy):
        copy.wait_send()

    for c in range(HALVES):
        each_send(me, c, 0, start)

    key_at = lax.broadcasted_iota(jnp.int32, (rows, rows), 0)
    query_at = lax.broadcasted_iota(jnp.int32, (rows, rows), 1)
    front[...] = jnp.zeros_like(front)
    back[...] = jnp.zeros_like(back)
    vt[:, dv:, :] = jnp.ones((groups, ONES, rows), jnp.bfloat16)

    vfew[:, dv:, :] = jnp.ones((groups, ONES, vfew.shape[2]), jnp.bfloat16)
    for copy in small:
        copy.wait()
    for g in range(groups):
        cols = slice(g * dq, (g + 1) * dq)
        pool_ref[:, cols] = poolk_ref[:, g, :]
        pool_ref[:, kcols + g * dv:kcols + (g + 1) * dv] = poolv_ref[:, g, :]
    for h in range(heads):
        ahead = ahead_of(h)
        empty = slice(dq, span) if ahead == 0 else slice(0, ahead)
        qt_ref[h, empty, :] = jnp.zeros((span - dq, rows), jnp.bfloat16)
    count_b = n_seq * blocks
    block_at = lax.broadcasted_iota(jnp.int32, (count_b, rows), 0)
    tile_at = lax.broadcasted_iota(jnp.int32, (1, rows), 1) // BLOCK
    for g in range(groups):
        listed = jnp.full((count_b, rows), NONE, jnp.float32)
        for e in range(list_ref.shape[2]):
            entry = jnp.full((1, rows), -1, jnp.int32)
            for t in range(tiles):
                entry = jnp.where(tile_at == t, list_ref[t, g, e], entry)
            listed = jnp.where(block_at == entry, 0.0, listed)
        bias_ref[g] = listed.reshape(n_seq, blocks, rows)
    for copy in asked:
        copy.wait()
    gated = gate_ref.shape[0]
    for h in range(heads):
        ahead = ahead_of(h)
        held_s[h * gated:(h + 1) * gated, :] = mm(gate_ref[...], qt_ref[h, ahead:ahead + dq, :])
    for h in range(heads):
        for b in range(gated // heads):
            at = h * gated + b * heads + h
            gates[h, b:b + 1, :] = jax.nn.sigmoid(held_s[at:at + 1, :])

    def chosen(cost):
        spans = [jnp.max(cost[c:c + 1], axis=1, keepdims=True) for c in range(blocks)]
        there = [jnp.where(top < 0.0, 0.0, 1.0) for top in spans]
        found = []
        for order in (range(blocks), range(blocks - 1, -1, -1)):
            left = jnp.ones_like(there[0])
            share = [None] * blocks
            for c in order:
                share[c] = left * there[c]
                left = left * (1.0 - there[c])
            found.append(share)
        number = sum(there)
        costs = [
            sum(w * cost[c:c + 1] for c, w in enumerate(share))
            + jnp.where(number > need, 0.0, NONE)
            for need, share in zip((0.5, 1.5), found)]
        return found, costs

    def update(h, scores, shift, acc, peak, values, first):
        tall = scores.shape[0]
        if shift is None:
            now = jnp.max(scores, axis=0, keepdims=True)
        else:
            scores = scores.reshape(shift.shape[0], BLOCK, rows)
            now = jnp.max(jnp.max(scores, axis=1) + shift, axis=0, keepdims=True)
        if not first:
            before = peak[h][0:1]
            now = jnp.maximum(before, now)
            shrink = jnp.exp2((before - now) * factor)
        if shift is None:
            raised = jnp.exp2((scores - now) * factor)
        else:
            raised = jnp.exp2((scores + (shift - now)[:, None, :]) * factor).reshape(tall, rows)
        fresh = mm(values, raised.astype(jnp.bfloat16))
        acc[h] = fresh if first else acc[h] * shrink + fresh
        peak[h] = jnp.broadcast_to(now, peak.shape[1:])

    def pool(s):
        raw = kv[s].astype(jnp.float32).reshape(per, STRIDE, kv.shape[2])
        at = pl.ds(pl.multiple_of(s * per, per), per)
        front[at, :] = jnp.sum(raw * pool_ref[:STRIDE][None], axis=1)
        back[at, :] = jnp.sum(raw * pool_ref[STRIDE:][None], axis=1)

    def whole(s, local):
        pool(s)
        gap = query_at - key_at if local else query_at + rows - key_at
        near[...] = jnp.where((gap >= 0) & (gap < WINDOW), 0.0, NONE)
        for g in range(groups):
            vt[g, :dv, :] = flip(kv[s, :, kcols + g * dv:kcols + (g + 1) * dv])
        for g in range(groups):
            kat = slice(g * LANES, g * LANES + span)
            for i in range(hpg):
                held_s[i * rows:(i + 1) * rows] = mm(kv[s, :, kat], qt_ref[g * hpg + i])
            for i in range(hpg):
                h = g * hpg + i
                scores = held_s[i * rows:(i + 1) * rows]
                close = scores + near[...]
                update(h, close if local else scores, bias_ref[g, s], acc_s, max_s, vt[g], local)
                update(h, close, None, acc_w, max_w, vt[g], local)

    def take(s, slot):
        pool(s)
        for g in range(groups):
            kat = slice(g * LANES, g * LANES + span)
            vat = slice(kcols + g * dv, kcols + (g + 1) * dv)
            found, costs = chosen(bias_ref[g, s])
            for c, (share, cost) in enumerate(zip(found, costs)):
                few_ref[g, slot * SLOTS + c:slot * SLOTS + c + 1, :] = cost

                def pick(cols):
                    parts = [
                        kv[s, b * BLOCK:(b + 1) * BLOCK, cols].astype(jnp.float32) * w
                        for b, w in enumerate(share)]
                    return sum(parts[1:], parts[0]).astype(jnp.bfloat16)

                kfew[g, slot * few + c * BLOCK:slot * few + (c + 1) * BLOCK, :] = pick(kat)
                held_v[g, c * BLOCK:(c + 1) * BLOCK, :] = pick(vat)
            vfew[g, :dv, slot * few:(slot + 1) * few] = flip(held_v[g])

    def attend(slots):
        tall = slots * few
        for g in range(groups):
            for i in range(hpg):
                held_s[i * rows:i * rows + tall] = mm(kfew[g, :tall], qt_ref[g * hpg + i])
            for i in range(hpg):
                h = g * hpg + i
                update(
                    h, held_s[i * rows:i * rows + tall], few_ref[g, :slots * SLOTS], acc_s, max_s,
                    vfew[g, :, :tall], False)

    whole(me, True)

    def step(k, carry):
        first = 2 * k - 1
        d = first // inner
        e = first % inner
        s1 = (z - d) * inner + (y + e) % inner
        d2 = (first + 1) // inner
        e2 = (first + 1) % inner
        s2 = (z - d2) * inner + (y + e2) % inner

        @pl.when((e == 1) & (d < z))
        def _():
            s3 = (z - d - 1) * inner + y
            for c in range(HALVES):
                arrive(s3, c)
                each_send(s3, c, d + 1, start)

        one = (d <= z) & (s1 < me)
        two = (first + 1 < n_seq) & (d2 <= z) & (s2 < me)
        close = one & (s1 == me - 1)
        far = one & (s1 != me - 1)

        @pl.when(one)
        def _():
            for c in range(HALVES):
                arrive(s1, c)

        @pl.when(two & (e2 != 0))
        def _():
            for c in range(HALVES):
                arrive(s2, c)

        @pl.when(close)
        def _():
            whole(s1, False)

        @pl.when(far & two)
        def _():
            take(s1, 0)
            take(s2, 1)
            attend(2)

        @pl.when(far != two)
        def _():
            take(jnp.where(far, s1, s2), 0)
            attend(1)

        return carry

    count = n_seq * per
    late = 2 * per
    last = 1 - y
    places = me * rows + lax.broadcasted_iota(jnp.int32, (1, rows), 1)
    tail = jnp.ones((ONES, count), jnp.bfloat16)
    batch = max(1, min(hpg, held_s.shape[0] // count))

    def hide(number, of_last):
        token = lax.broadcasted_iota(jnp.int32, (number, rows), 0)
        seen = token * STRIDE + (CBLOCK - 1) <= places
        if both_ways:
            touched = (token >= last * per - 1) & (token < (last + 1) * per)
            seen = seen & (touched if of_last else jnp.logical_not(touched))
        return jnp.where(seen, 0.0, NONE)

    def compressed():
        packed = (front[...] + back[pl.ds(1, count), :]).astype(jnp.bfloat16)
        hidden = hide(count, False)
        for g in range(groups):
            pooled_k = packed[:, g * LANES:g * LANES + span]
            pooled_v = flip(packed[:, kcols + g * dv:kcols + (g + 1) * dv])
            pooled_v = jnp.concatenate([pooled_v, tail], 0)
            for i in range(hpg):
                h = g * hpg + i
                if i % batch == 0:
                    for u in range(batch):
                        held_s[u * count:(u + 1) * count] = mm(pooled_k, qt_ref[h + u])
                scores = held_s[i % batch * count:(i % batch + 1) * count] + hidden
                top = jnp.maximum(jnp.max(scores, axis=0, keepdims=True), FLOOR)
                raised = jnp.exp2((scores - top) * factor).astype(jnp.bfloat16)
                acc_c[h] = mm(pooled_v, raised)
                max_c[h] = jnp.broadcast_to(top, max_c.shape[1:])

    def rest(tall):
        packed = (front[:late] + back[1:late + 1]).astype(jnp.bfloat16)
        hidden = hide(late, True)
        for g in range(groups):
            kfew[g, few:few + late, :] = packed[:, g * LANES:g * LANES + span]
            vfew[g, :dv, few:few + late] = flip(packed[:, kcols + g * dv:kcols + (g + 1) * dv])
        for g in range(groups):
            for i in range(hpg):
                held_s[i * rows:i * rows + tall + late] = mm(kfew[g, few - tall:few + late], qt_ref[g * hpg + i])
            for i in range(hpg):
                h = g * hpg + i
                if tall:
                    update(
                        h, held_s[i * rows:i * rows + tall], few_ref[g, :SLOTS], acc_s, max_s,
                        vfew[g, :, :tall], False)
                update(
                    h, held_s[i * rows + tall:i * rows + tall + late] + hidden, None, acc_c, max_c,
                    vfew[g, :, few:few + late], False)

    if both_ways:
        lax.fori_loop(1, z + 1, step, 0)
        compressed()
        arrive(last, HALVES - 1)
        up(last, HALVES - 1, start)

        @pl.when(me > 0)
        def _():
            for c in range(HALVES - 1):
                arrive(last, c)

        @pl.when((me > 0) & (last == me - 1))
        def _():
            whole(last, False)
            rest(0)

        @pl.when((me > 0) & (last != me - 1))
        def _():
            take(last, 0)
            rest(few)
    else:
        lax.fori_loop(1, n_seq // 2 + 1, step, 0)
        compressed()

    for h in range(heads):
        gate = gates[h]
        total = jnp.zeros((dv, rows), jnp.float32)
        for b, found in enumerate((acc_c[h], acc_s[h], acc_w[h])):
            share = gate[b:b + 1] / jnp.maximum(found[dv:dv + 1], 1.0)
            total = total + found[:dv] * share
        mixed[h * dv:(h + 1) * dv, :] = total.astype(jnp.bfloat16)

    weights.wait()
    pieces = outgo.shape[0]
    wide = outgo.shape[1]
    half = pieces * wide

    def swap(j):
        return pltpu.make_async_remote_copy(
            src_ref=outgo.at[j], dst_ref=incoming.at[j], send_sem=psend.at[j],
            recv_sem=precv.at[j], device_id=(part, me, 1 - side), device_id_type=MESH)

    def project(to, j):
        at = pl.ds(pl.multiple_of(to * half + j * wide, wide), wide)
        return mm(w[at, :], mixed[...])

    for j in range(pieces):
        outgo[j] = project(1 - side, j).astype(jnp.bfloat16)
    for j in range(pieces):
        swap(j).start()
    for j in range(pieces):
        held_p[j] = project(side, j)
    for j in range(pieces):
        swap(j).wait_recv()
    for j in range(pieces):
        both = held_p[j] + incoming[j].astype(jnp.float32)
        out_ref[:, j * wide:(j + 1) * wide] = jnp.transpose(both).astype(jnp.bfloat16)
    for j in range(pieces):
        swap(j).wait_send()
    for c in range(HALVES):
        each_send(me, c, 0, sent)

    def drain(d, carry):
        @pl.when(d <= z)
        def _():
            for c in range(HALVES):
                each_send((z - d) * inner + y, c, d, sent)

        return carry

    lax.fori_loop(1, outer, drain, 0)
    if both_ways:
        up(1 - y, HALVES - 1, sent)


def solution(mesh):
    n_seq = mesh.shape["seq"]
    inner = 2
    while inner * inner * 4 <= n_seq:
        inner *= 2

    def shards(queries, keys, values, lists, gate_weight, pool_key, pool_value, out_weight):
        rows, heads, dq = queries.shape
        groups = keys.shape[1]
        dv = values.shape[2]
        assert groups == 2 and groups * (dq - LANES) == LANES and rows >= WINDOW
        kcols = groups * dq
        kt = jnp.transpose(keys, (1, 2, 0)).reshape(kcols, rows)
        flat = values.reshape(rows * groups, dv)
        span = 2 * LANES
        qt = jnp.transpose(queries, (1, 2, 0))
        gw = jnp.transpose(gate_weight, (2, 0, 1)).reshape(-1, dq)
        blocks = rows // BLOCK
        width = kcols + groups * dv
        d_out, d_in = out_weight.shape
        half = d_out // 2
        wide = half // 2
        vmem = pl.BlockSpec(memory_space=pltpu.VMEM)
        hbm = pl.BlockSpec(memory_space=pltpu.HBM)
        dma = pltpu.SemaphoreType.DMA
        per = rows // STRIDE
        return pl.pallas_call(
            functools.partial(kernel, n_seq, inner, dq ** -0.5 * math.log2(math.e), kcols),
            out_shape=jax.ShapeDtypeStruct((rows, half), jnp.bfloat16),
            in_specs=[hbm] * 8,
            out_specs=vmem,
            scratch_shapes=[
                pltpu.VMEM((n_seq, rows, width), jnp.bfloat16),
                pltpu.VMEM((d_out, d_in), jnp.bfloat16),
                pltpu.VMEM((heads, span, rows), jnp.bfloat16),
                pltpu.VMEM((groups, n_seq, blocks, rows), jnp.float32),
                pltpu.VMEM((CBLOCK, width), jnp.float32),
                pltpu.VMEM((heads, dv + ONES, rows), jnp.float32),
                pltpu.VMEM((heads, dv + ONES, rows), jnp.float32),
                pltpu.VMEM((heads, 8, rows), jnp.float32),
                pltpu.VMEM((heads, 8, rows), jnp.float32),
                pltpu.VMEM((groups, dv + ONES, rows), jnp.bfloat16),
                pltpu.VMEM((rows, rows), jnp.float32),
                pltpu.VMEM((n_seq * per, width), jnp.float32),
                pltpu.VMEM((n_seq * per + 8, width), jnp.float32),
                pltpu.VMEM((d_in, rows), jnp.bfloat16),
                pltpu.VMEM((heads, 8, rows), jnp.float32),
                pltpu.VMEM((groups, SLOTS * BLOCK, dv), jnp.bfloat16),
                pltpu.VMEM((groups, 2 * SLOTS, rows), jnp.float32),
                pltpu.VMEM((groups, 2 * SLOTS * BLOCK, span), jnp.bfloat16),
                pltpu.VMEM((groups, dv + ONES, 2 * SLOTS * BLOCK), jnp.bfloat16),
                pltpu.VMEM((half // wide, wide, rows), jnp.bfloat16),
                pltpu.VMEM((half // wide, wide, rows), jnp.bfloat16),
                pltpu.VMEM((max(heads // groups * rows, n_seq * per), rows), jnp.float32),
                pltpu.VMEM((half // wide, wide, rows), jnp.float32),
                pltpu.VMEM((kcols, rows), jnp.bfloat16),
                pltpu.VMEM((rows * groups, dv), jnp.bfloat16),
                pltpu.VMEM((rows, rows), jnp.bfloat16),
                pltpu.VMEM((heads, dv + ONES, rows), jnp.float32),
                pltpu.VMEM((heads, 8, rows), jnp.float32),
                pltpu.SMEM(lists.shape, jnp.int32),
                pltpu.VMEM(gw.shape, jnp.bfloat16),
                pltpu.VMEM(pool_key.shape, jnp.float32),
                pltpu.VMEM(pool_value.shape, jnp.float32),
                dma((2,)), dma((4,)), dma((groups,)), dma, dma((n_seq, HALVES)), dma((n_seq, HALVES, inner)), dma((n_seq, HALVES)),
                dma((half // wide,)), dma((half // wide,)),
            ],
            compiler_params=pltpu.CompilerParams(
                collective_id=0, has_side_effects=True, vmem_limit_bytes=(50 if n_seq <= 8 else 61) * 1024 * 1024),
        )(*(pltpu.with_memory_space_constraint(a, pltpu.HBM) for a in (kt, flat, qt, lists, gw, pool_key, pool_value, out_weight)))

    return jax.shard_map(
        shards,
        mesh=mesh,
        in_specs=(
            P(("groups", "seq"), "head", None),
            P(("groups", "seq"), "head", None),
            P(("groups", "seq"), "head", None),
            P(("groups", "seq"), "head", None),
            P("head", None, None),
            P(None, "head", None),
            P(None, "head", None),
            P(None, "head"),
        ),
        out_specs=P(("groups", "seq"), "head"),
        check_vma=False,
    )
```

```python
import functools
import math

import jax
import jax.numpy as jnp
from jax import lax
from jax.experimental import pallas as pl
from jax.experimental.pallas import tpu as pltpu
from jax.sharding import PartitionSpec as P

BLOCK = 64
CBLOCK = 32
STRIDE = 16
WINDOW = 256
SLOTS = 2
LANES = 128
NONE = -1e30
FLOOR = -1e6
ONES = 16
HALVES = 2
MESH = pl.DeviceIdType.MESH


def mm(a, b):
    return jnp.dot(a, b, preferred_element_type=jnp.float32)


def nt(a, b):
    return lax.dot_general(a, b, (((1,), (1,)), ((), ())), preferred_element_type=jnp.float32)


def kernel(
    n_seq, inner, factor, kcols,
    keys_ref, values_ref, queries_ref, lists_ref, gates_ref, poolks_ref, poolvs_ref, w_ref, out_ref,
    kv, w, qt_ref, bias_ref, pool_ref, acc_s, acc_w, max_s, max_w, vt, near, front, back, mixed, gates, held_v, few_ref, kfew, vfew,
    outgo, incoming, held_s, held_p, kraw, vraw, eye, acc_c, max_c,
    list_ref, gate_ref, poolk_ref, poolv_ref,
    own_sem, small_sem, query_sem, w_sem, zsend, ysend, recv, psend, precv,
):
    outer = n_seq // inner
    rows = kv.shape[1]
    heads = qt_ref.shape[0]
    groups = list_ref.shape[1]
    dq = queries_ref.shape[1]
    tiles = list_ref.shape[0]
    hpg = heads // groups
    dv = acc_s.shape[1] - ONES
    span = 2 * LANES
    blocks = rows // BLOCK
    per = rows // STRIDE
    few = SLOTS * BLOCK
    both_ways = inner == 2
    me = lax.axis_index("seq")
    part = lax.axis_index("groups")
    side = lax.axis_index("head")
    z = me // inner
    y = me % inner

    own = [pltpu.make_async_copy(a, b, own_sem.at[i])
           for i, (a, b) in enumerate(((keys_ref, kraw), (values_ref, vraw)))]
    for copy in own:
        copy.start()

    barrier = pltpu.get_barrier_semaphore()

    def greet(who, hd):
        pl.semaphore_signal(barrier, inc=1, device_id=(part, who, hd), device_id_type=MESH)

    greet(me, 1 - side)

    @pl.when(z > 0)
    def _():
        greet(me - inner, side)

    @pl.when(z < outer - 1)
    def _():
        greet(me + inner, side)

    for e in range(1, inner):
        greet(z * inner + (y + e) % inner, side)

    def ahead_of(h):
        return (h // hpg) * (dq - LANES)

    small = [pltpu.make_async_copy(a, b, small_sem.at[i]) for i, (a, b) in enumerate((
        (lists_ref, list_ref), (gates_ref, gate_ref), (poolks_ref, poolk_ref), (poolvs_ref, poolv_ref)))]
    for copy in small:
        copy.start()
    asked = [pltpu.make_async_copy(
        queries_ref.at[g * hpg:(g + 1) * hpg],
        qt_ref.at[g * hpg:(g + 1) * hpg, ahead_of(g * hpg):ahead_of(g * hpg) + dq], query_sem.at[g])
        for g in range(groups)]
    for copy in asked:
        copy.start()
    weights = pltpu.make_async_copy(w_ref, w, w_sem)
    weights.start()

    spot = lax.broadcasted_iota(jnp.int32, (rows, rows), 0)
    eye[...] = jnp.where(spot == lax.broadcasted_iota(jnp.int32, (rows, rows), 1), 1.0, 0.0).astype(jnp.bfloat16)
    from_row = lax.broadcasted_iota(jnp.int32, (rows, rows * groups), 0) * groups
    from_col = lax.broadcasted_iota(jnp.int32, (rows, rows * groups), 1)

    def flip(a):
        n = a.shape[1]
        return nt(eye[:n, :n], a).astype(jnp.bfloat16)

    own[0].wait()
    for g in range(groups):
        kv[me, :, g * dq:(g + 1) * dq] = nt(eye[...], kraw[g * dq:(g + 1) * dq, :]).astype(jnp.bfloat16)
    own[1].wait()
    for g in range(groups):
        pull = jnp.where(from_col == from_row + g, 1.0, 0.0).astype(jnp.bfloat16)
        kv[me, :, kcols + g * dv:kcols + (g + 1) * dv] = mm(pull, vraw[...]).astype(jnp.bfloat16)

    lower = jnp.minimum(z, 1)
    upper = jnp.minimum(outer - 1 - z, 1)
    pl.semaphore_wait(barrier, inner + lower + upper)

    size = rows // HALVES

    def along(s, c):
        return pltpu.make_async_remote_copy(
            src_ref=kv.at[s, c * size:(c + 1) * size], dst_ref=kv.at[s, c * size:(c + 1) * size],
            send_sem=zsend.at[s, c], recv_sem=recv.at[s, c],
            device_id=(part, me + inner, side), device_id_type=MESH)

    def across(s, c, e):
        return pltpu.make_async_remote_copy(
            src_ref=kv.at[s, c * size:(c + 1) * size], dst_ref=kv.at[s, c * size:(c + 1) * size],
            send_sem=ysend.at[s, c, e], recv_sem=recv.at[s, c],
            device_id=(part, z * inner + (y + e) % inner, side), device_id_type=MESH)

    def up(s, c, act):
        @pl.when(z < outer - 1)
        def _():
            act(along(s, c))

    def each_send(s, c, d, act):
        up(s, c, act)
        for e in range(1, inner):
            wanted = (d > 0) | (y + e < inner)
            if both_ways and c == HALVES - 1:
                wanted = (wanted & (d < z)) | (z == 0)

            @pl.when(wanted)
            def _():
                act(across(s, c, e))

    def arrive(s, c):
        pltpu.make_async_remote_copy(
            src_ref=kv.at[s, c * size:(c + 1) * size], dst_ref=kv.at[s, c * size:(c + 1) * size],
            send_sem=zsend.at[s, c], recv_sem=recv.at[s, c],
            device_id=(part, me, 1 - side), device_id_type=MESH).wait_recv()

    def start(copy):
        copy.start()

    def sent(copy):
        copy.wait_send()

    for c in range(HALVES):
        each_send(me, c, 0, start)

    key_at = lax.broadcasted_iota(jnp.int32, (rows, rows), 0)
    query_at = lax.broadcasted_iota(jnp.int32, (rows, rows), 1)
    front[...] = jnp.zeros_like(front)
    back[...] = jnp.zeros_like(back)
    vt[:, dv:, :] = jnp.ones((groups, ONES, rows), jnp.bfloat16)

    vfew[:, dv:, :] = jnp.ones((groups, ONES, vfew.shape[2]), jnp.bfloat16)
    for copy in small:
        copy.wait()
    for g in range(groups):
        cols = slice(g * dq, (g + 1) * dq)
        pool_ref[:, cols] = poolk_ref[:, g, :]
        pool_ref[:, kcols + g * dv:kcols + (g + 1) * dv] = poolv_ref[:, g, :]
    for h in range(heads):
        ahead = ahead_of(h)
        empty = slice(dq, span) if ahead == 0 else slice(0, ahead)
        qt_ref[h, empty, :] = jnp.zeros((span - dq, rows), jnp.bfloat16)
    count_b = n_seq * blocks
    block_at = lax.broadcasted_iota(jnp.int32, (count_b, rows), 0)
    tile_at = lax.broadcasted_iota(jnp.int32, (1, rows), 1) // BLOCK
    for g in range(groups):
        listed = jnp.full((count_b, rows), NONE, jnp.float32)
        for e in range(list_ref.shape[2]):
            entry = jnp.full((1, rows), -1, jnp.int32)
            for t in range(tiles):
                entry = jnp.where(tile_at == t, list_ref[t, g, e], entry)
            listed = jnp.where(block_at == entry, 0.0, listed)
        bias_ref[g] = listed.reshape(n_seq, blocks, rows)
    for copy in asked:
        copy.wait()
    gated = gate_ref.shape[0]
    for h in range(heads):
        ahead = ahead_of(h)
        held_s[h * gated:(h + 1) * gated, :] = mm(gate_ref[...], qt_ref[h, ahead:ahead + dq, :])
    for h in range(heads):
        for b in range(gated // heads):
            at = h * gated + b * heads + h
            gates[h, b:b + 1, :] = jax.nn.sigmoid(held_s[at:at + 1, :])

    def chosen(cost):
        spans = [jnp.max(cost[c:c + 1], axis=1, keepdims=True) for c in range(blocks)]
        there = [jnp.where(top < 0.0, 0.0, 1.0) for top in spans]
        found = []
        for order in (range(blocks), range(blocks - 1, -1, -1)):
            left = jnp.ones_like(there[0])
            share = [None] * blocks
            for c in order:
                share[c] = left * there[c]
                left = left * (1.0 - there[c])
            found.append(share)
        number = sum(there)
        costs = [
            sum(w * cost[c:c + 1] for c, w in enumerate(share))
            + jnp.where(number > need, 0.0, NONE)
            for need, share in zip((0.5, 1.5), found)]
        return found, costs

    def update(h, scores, shift, acc, peak, values, first):
        tall = scores.shape[0]
        if shift is None:
            now = jnp.max(scores, axis=0, keepdims=True)
        else:
            scores = scores.reshape(shift.shape[0], BLOCK, rows)
            now = jnp.max(jnp.max(scores, axis=1) + shift, axis=0, keepdims=True)
        if not first:
            before = peak[h][0:1]
            now = jnp.maximum(before, now)
            shrink = jnp.exp2((before - now) * factor)
        if shift is None:
            raised = jnp.exp2((scores - now) * factor)
        else:
            raised = jnp.exp2((scores + (shift - now)[:, None, :]) * factor).reshape(tall, rows)
        fresh = mm(values, raised.astype(jnp.bfloat16))
        acc[h] = fresh if first else acc[h] * shrink + fresh
        peak[h] = jnp.broadcast_to(now, peak.shape[1:])

    def pool(s):
        raw = kv[s].astype(jnp.float32).reshape(per, STRIDE, kv.shape[2])
        at = pl.ds(pl.multiple_of(s * per, per), per)
        front[at, :] = jnp.sum(raw * pool_ref[:STRIDE][None], axis=1)
        back[at, :] = jnp.sum(raw * pool_ref[STRIDE:][None], axis=1)

    def whole(s, local):
        pool(s)
        gap = query_at - key_at if local else query_at + rows - key_at
        near[...] = jnp.where((gap >= 0) & (gap < WINDOW), 0.0, NONE)
        for g in range(groups):
            vt[g, :dv, :] = flip(kv[s, :, kcols + g * dv:kcols + (g + 1) * dv])
        for g in range(groups):
            kat = slice(g * LANES, g * LANES + span)
            for i in range(hpg):
                held_s[i * rows:(i + 1) * rows] = mm(kv[s, :, kat], qt_ref[g * hpg + i])
            for i in range(hpg):
                h = g * hpg + i
                scores = held_s[i * rows:(i + 1) * rows]
                close = scores + near[...]
                update(h, close if local else scores, bias_ref[g, s], acc_s, max_s, vt[g], local)
                update(h, close, None, acc_w, max_w, vt[g], local)

    def take(s, slot):
        pool(s)
        for g in range(groups):
            kat = slice(g * LANES, g * LANES + span)
            vat = slice(kcols + g * dv, kcols + (g + 1) * dv)
            found, costs = chosen(bias_ref[g, s])
            for c, (share, cost) in enumerate(zip(found, costs)):
                few_ref[g, slot * SLOTS + c:slot * SLOTS + c + 1, :] = cost

                def pick(cols):
                    parts = [
                        kv[s, b * BLOCK:(b + 1) * BLOCK, cols].astype(jnp.float32) * w
                        for b, w in enumerate(share)]
                    return sum(parts[1:], parts[0]).astype(jnp.bfloat16)

                kfew[g, slot * few + c * BLOCK:slot * few + (c + 1) * BLOCK, :] = pick(kat)
                held_v[g, c * BLOCK:(c + 1) * BLOCK, :] = pick(vat)
            vfew[g, :dv, slot * few:(slot + 1) * few] = flip(held_v[g])

    def attend(slots):
        tall = slots * few
        for g in range(groups):
            for i in range(hpg):
                held_s[i * rows:i * rows + tall] = mm(kfew[g, :tall], qt_ref[g * hpg + i])
            for i in range(hpg):
                h = g * hpg + i
                update(
                    h, held_s[i * rows:i * rows + tall], few_ref[g, :slots * SLOTS], acc_s, max_s,
                    vfew[g, :, :tall], False)

    count = n_seq * per
    late = 2 * per
    last = 1 - y
    places = me * rows + lax.broadcasted_iota(jnp.int32, (1, rows), 1)
    tail = jnp.ones((ONES, count), jnp.bfloat16)
    batch = max(1, min(hpg, held_s.shape[0] // count))

    def hide(number, of_last):
        token = lax.broadcasted_iota(jnp.int32, (number, rows), 0)
        seen = token * STRIDE + (CBLOCK - 1) <= places
        if both_ways:
            touched = (token >= last * per - 1) & (token < (last + 1) * per)
            seen = seen & (touched if of_last else jnp.logical_not(touched))
        return jnp.where(seen, 0.0, NONE)

    def compressed():
        packed = (front[...] + back[pl.ds(1, count), :]).astype(jnp.bfloat16)
        hidden = hide(count, False)
        for g in range(groups):
            pooled_k = packed[:, g * LANES:g * LANES + span]
            pooled_v = flip(packed[:, kcols + g * dv:kcols + (g + 1) * dv])
            pooled_v = jnp.concatenate([pooled_v, tail], 0)
            for i in range(hpg):
                h = g * hpg + i
                if i % batch == 0:
                    for u in range(batch):
                        held_s[u * count:(u + 1) * count] = mm(pooled_k, qt_ref[h + u])
                scores = held_s[i % batch * count:(i % batch + 1) * count] + hidden
                top = jnp.maximum(jnp.max(scores, axis=0, keepdims=True), FLOOR)
                raised = jnp.exp2((scores - top) * factor).astype(jnp.bfloat16)
                acc_c[h] = mm(pooled_v, raised)
                max_c[h] = jnp.broadcast_to(top, max_c.shape[1:])

    def rest(tall):
        packed = (front[:late] + back[1:late + 1]).astype(jnp.bfloat16)
        hidden = hide(late, True)
        for g in range(groups):
            kfew[g, few:few + late, :] = packed[:, g * LANES:g * LANES + span]
            vfew[g, :dv, few:few + late] = flip(packed[:, kcols + g * dv:kcols + (g + 1) * dv])
        for g in range(groups):
            for i in range(hpg):
                held_s[i * rows:i * rows + tall + late] = mm(kfew[g, few - tall:few + late], qt_ref[g * hpg + i])
            for i in range(hpg):
                h = g * hpg + i
                if tall:
                    update(
                        h, held_s[i * rows:i * rows + tall], few_ref[g, :SLOTS], acc_s, max_s,
                        vfew[g, :, :tall], False)
                update(
                    h, held_s[i * rows + tall:i * rows + tall + late] + hidden, None, acc_c, max_c,
                    vfew[g, :, few:few + late], False)

    def attend_all():
        tall = 2 * few
        high = tall + count
        packed = (front[...] + back[pl.ds(1, count), :]).astype(jnp.bfloat16)
        hidden = hide(count, False)
        for g in range(groups):
            kfew[g, tall:high, :] = packed[:, g * LANES:g * LANES + span]
            pooled_v = flip(packed[:, kcols + g * dv:kcols + (g + 1) * dv])
            pooled_v = jnp.concatenate([pooled_v, tail], 0)
            for i in range(hpg):
                held_s[i * high:(i + 1) * high] = mm(kfew[g], qt_ref[g * hpg + i])
            for i in range(hpg):
                h = g * hpg + i
                update(
                    h, held_s[i * high:i * high + tall], few_ref[g], acc_s, max_s, vfew[g, :, :tall], False)
                scores = held_s[i * high + tall:(i + 1) * high] + hidden
                top = jnp.maximum(jnp.max(scores, axis=0, keepdims=True), FLOOR)
                raised = jnp.exp2((scores - top) * factor).astype(jnp.bfloat16)
                acc_c[h] = mm(pooled_v, raised)
                max_c[h] = jnp.broadcast_to(top, max_c.shape[1:])

    whole(me, True)

    def step(k, carry):
        first = 2 * k - 1
        d = first // inner
        e = first % inner
        s1 = (z - d) * inner + (y + e) % inner
        d2 = (first + 1) // inner
        e2 = (first + 1) % inner
        s2 = (z - d2) * inner + (y + e2) % inner

        s3 = (z - d - 1) * inner + y
        one = (d <= z) & (s1 < me)
        two = (first + 1 < n_seq) & (d2 <= z) & (s2 < me)
        close = one & (s1 == me - 1)
        far = one & (s1 != me - 1)

        def pass_on(c):
            @pl.when((e == 1) & (d < z))
            def _():
                arrive(s3, c)
                each_send(s3, c, d + 1, start)

        for c in range(HALVES - 1):
            pass_on(c)

        @pl.when(one)
        def _():
            for c in range(HALVES):
                arrive(s1, c)

        @pl.when(far & two)
        def _():
            take(s1, 0)

        pass_on(HALVES - 1)

        @pl.when(two & (e2 != 0))
        def _():
            for c in range(HALVES):
                arrive(s2, c)

        @pl.when(close)
        def _():
            whole(s1, False)

        @pl.when(far & two)
        def _():
            take(s2, 1)

        @pl.when(far & two & ((k < z) if both_ways else True))
        def _():
            attend(2)

        if both_ways:
            @pl.when(far & two & (k == z))
            def _():
                attend_all()

        @pl.when(far != two)
        def _():
            take(jnp.where(far, s1, s2), 0)
            attend(1)

        return carry

    if both_ways:
        lax.fori_loop(1, z + 1, step, 0)

        @pl.when((z == 0) | (inner + last >= me - 1))
        def _():
            compressed()

        arrive(last, HALVES - 1)
        up(last, HALVES - 1, start)

        @pl.when(me > 0)
        def _():
            for c in range(HALVES - 1):
                arrive(last, c)

        @pl.when((me > 0) & (last == me - 1))
        def _():
            whole(last, False)
            rest(0)

        @pl.when((me > 0) & (last != me - 1))
        def _():
            take(last, 0)
            rest(few)
    else:
        lax.fori_loop(1, n_seq // 2 + 1, step, 0)
        compressed()

    for h in range(heads):
        gate = gates[h]
        total = jnp.zeros((dv, rows), jnp.float32)
        for b, found in enumerate((acc_c[h], acc_s[h], acc_w[h])):
            share = gate[b:b + 1] / jnp.maximum(found[dv:dv + 1], 1.0)
            total = total + found[:dv] * share
        mixed[h * dv:(h + 1) * dv, :] = total.astype(jnp.bfloat16)

    weights.wait()
    pieces = outgo.shape[0]
    wide = outgo.shape[1]
    half = pieces * wide

    def swap(j):
        return pltpu.make_async_remote_copy(
            src_ref=outgo.at[j], dst_ref=incoming.at[j], send_sem=psend.at[j],
            recv_sem=precv.at[j], device_id=(part, me, 1 - side), device_id_type=MESH)

    def project(to, j):
        at = pl.ds(pl.multiple_of(to * half + j * wide, wide), wide)
        return mm(w[at, :], mixed[...])

    for j in range(pieces):
        outgo[j] = project(1 - side, j).astype(jnp.bfloat16)
    for j in range(pieces):
        swap(j).start()
    for j in range(pieces):
        held_p[j] = project(side, j)
    for j in range(pieces):
        swap(j).wait_recv()
    for j in range(pieces):
        both = held_p[j] + incoming[j].astype(jnp.float32)
        out_ref[:, j * wide:(j + 1) * wide] = jnp.transpose(both).astype(jnp.bfloat16)
    for j in range(pieces):
        swap(j).wait_send()
    for c in range(HALVES):
        each_send(me, c, 0, sent)

    def drain(d, carry):
        @pl.when(d <= z)
        def _():
            for c in range(HALVES):
                each_send((z - d) * inner + y, c, d, sent)

        return carry

    lax.fori_loop(1, outer, drain, 0)
    if both_ways:
        up(1 - y, HALVES - 1, sent)


def solution(mesh):
    n_seq = mesh.shape["seq"]
    inner = 2
    while inner * inner * 4 <= n_seq:
        inner *= 2

    def shards(queries, keys, values, lists, gate_weight, pool_key, pool_value, out_weight):
        rows, heads, dq = queries.shape
        groups = keys.shape[1]
        dv = values.shape[2]
        assert groups == 2 and groups * (dq - LANES) == LANES and rows >= WINDOW
        kcols = groups * dq
        kt = jnp.transpose(keys, (1, 2, 0)).reshape(kcols, rows)
        flat = values.reshape(rows * groups, dv)
        span = 2 * LANES
        qt = jnp.transpose(queries, (1, 2, 0))
        gw = jnp.transpose(gate_weight, (2, 0, 1)).reshape(-1, dq)
        blocks = rows // BLOCK
        width = kcols + groups * dv
        d_out, d_in = out_weight.shape
        half = d_out // 2
        wide = half // 2
        vmem = pl.BlockSpec(memory_space=pltpu.VMEM)
        hbm = pl.BlockSpec(memory_space=pltpu.HBM)
        dma = pltpu.SemaphoreType.DMA
        per = rows // STRIDE
        return pl.pallas_call(
            functools.partial(kernel, n_seq, inner, dq ** -0.5 * math.log2(math.e), kcols),
            out_shape=jax.ShapeDtypeStruct((rows, half), jnp.bfloat16),
            in_specs=[hbm] * 8,
            out_specs=vmem,
            scratch_shapes=[
                pltpu.VMEM((n_seq, rows, width), jnp.bfloat16),
                pltpu.VMEM((d_out, d_in), jnp.bfloat16),
                pltpu.VMEM((heads, span, rows), jnp.bfloat16),
                pltpu.VMEM((groups, n_seq, blocks, rows), jnp.float32),
                pltpu.VMEM((CBLOCK, width), jnp.float32),
                pltpu.VMEM((heads, dv + ONES, rows), jnp.float32),
                pltpu.VMEM((heads, dv + ONES, rows), jnp.float32),
                pltpu.VMEM((heads, 8, rows), jnp.float32),
                pltpu.VMEM((heads, 8, rows), jnp.float32),
                pltpu.VMEM((groups, dv + ONES, rows), jnp.bfloat16),
                pltpu.VMEM((rows, rows), jnp.float32),
                pltpu.VMEM((n_seq * per, width), jnp.float32),
                pltpu.VMEM((n_seq * per + 8, width), jnp.float32),
                pltpu.VMEM((d_in, rows), jnp.bfloat16),
                pltpu.VMEM((heads, 8, rows), jnp.float32),
                pltpu.VMEM((groups, SLOTS * BLOCK, dv), jnp.bfloat16),
                pltpu.VMEM((groups, 2 * SLOTS, rows), jnp.float32),
                pltpu.VMEM((groups, 2 * SLOTS * BLOCK + (n_seq * per if inner == 2 else 0), span), jnp.bfloat16),
                pltpu.VMEM((groups, dv + ONES, 2 * SLOTS * BLOCK), jnp.bfloat16),
                pltpu.VMEM((half // wide, wide, rows), jnp.bfloat16),
                pltpu.VMEM((half // wide, wide, rows), jnp.bfloat16),
                pltpu.VMEM((max(heads // groups * (rows + (n_seq * per if inner == 2 else 0)), n_seq * per), rows), jnp.float32),
                pltpu.VMEM((half // wide, wide, rows), jnp.float32),
                pltpu.VMEM((kcols, rows), jnp.bfloat16),
                pltpu.VMEM((rows * groups, dv), jnp.bfloat16),
                pltpu.VMEM((rows, rows), jnp.bfloat16),
                pltpu.VMEM((heads, dv + ONES, rows), jnp.float32),
                pltpu.VMEM((heads, 8, rows), jnp.float32),
                pltpu.SMEM(lists.shape, jnp.int32),
                pltpu.VMEM(gw.shape, jnp.bfloat16),
                pltpu.VMEM(pool_key.shape, jnp.float32),
                pltpu.VMEM(pool_value.shape, jnp.float32),
                dma((2,)), dma((4,)), dma((groups,)), dma, dma((n_seq, HALVES)), dma((n_seq, HALVES, inner)), dma((n_seq, HALVES)),
                dma((half // wide,)), dma((half // wide,)),
            ],
            compiler_params=pltpu.CompilerParams(
                collective_id=0, has_side_effects=True, vmem_limit_bytes=(50 if n_seq <= 8 else 61) * 1024 * 1024),
        )(*(pltpu.with_memory_space_constraint(a, pltpu.HBM) for a in (kt, flat, qt, lists, gw, pool_key, pool_value, out_weight)))

    return jax.shard_map(
        shards,
        mesh=mesh,
        in_specs=(
            P(("groups", "seq"), "head", None),
            P(("groups", "seq"), "head", None),
            P(("groups", "seq"), "head", None),
            P(("groups", "seq"), "head", None),
            P("head", None, None),
            P(None, "head", None),
            P(None, "head", None),
            P(None, "head"),
        ),
        out_specs=P(("groups", "seq"), "head"),
        check_vma=False,
    )
```
